256 devices in a mesh: dp: 8 (over y, core), ctx: 32 (over z, x).
Axes of the slice: x: 4, y: 4, z: 8, core: 2. Of those that a mesh axis runs over, the one named last changes fastest.
Arguments:
- q_in: bfloat16 [65536, 1024], P(('dp', 'ctx')), may hold values from -5 to 5
- k_in: bfloat16 [65536, 1024], P(('dp', 'ctx')), may hold values from -5 to 5
- v_in: bfloat16 [65536, 1024], P(('dp', 'ctx')), may hold values from -6 to 6
- cotangent: bfloat16 [65536, 2048], P(('dp', 'ctx')), may hold values from -1.796875 to 1.796875
- out_weight: bfloat16 [1024, 2048], replicated, may hold values from -0.1875 to 0.1875
- cluster_ids: int32 [8, 65536, 1], P(None, ('dp', 'ctx')), may hold values from 0 to 63; in each aligned block of 256 rows (0 to 255, 256 to 511, ..., all dimensions but the last counted through in order) at most 8 rows name the same one
Outputs:
- layer_out: bfloat16 [65536, 2048], P(('dp', 'ctx'))
- q_grad: bfloat16 [65536, 1024], P(('dp', 'ctx'))
- k_grad: bfloat16 [65536, 1024], P(('dp', 'ctx'))
- v_grad: bfloat16 [65536, 1024], P(('dp', 'ctx'))
- wo_grad: float32 [1024, 2048], P('ctx')
The draws below stay inside these ranges and needn't reach their ends.
Inputs may be any that keep to these rules, and one draw needn't show every extreme that they name: `cluster_ids`: for each head, the 256 tokens of one device name any one cluster at most 8 times, a bound that some block reaches.
All inputs are finite; a program needn't handle non-finite values.
Results may differ from the reference program's by a relative error of at most 0.0085.
Values may be sent and summed in bfloat16 or wider, within the bound.
No kernel may reach another device: no remote copies, remote signals or barrier semaphores. Data moves between devices by JAX's collectives and lax.ppermute only.
A program may use at most 128 MiB of HBM per device.

```python
import math
import jax
import jax.numpy as jnp
import numpy as np
from jax import lax

D = 2048
HEADS = 8
HEAD_DIM = 128
TOK_DEV = 256
CLUSTERS = 64
CAP = 8
TOKENS = 65536
LENGTH = 8192


def rough_rows(key, salt):
    sub_key = jax.random.fold_in(key, salt)
    entries = jnp.clip(jax.random.normal(sub_key, (TOKENS, HEADS, HEAD_DIM)), -4.0, 4.0)
    return entries.astype(jnp.float32).reshape(TOKENS, HEADS * HEAD_DIM).astype(jnp.bfloat16)


def draw_q_in(key, part):
    return rough_rows(key, 22)


def draw_k_in(key, part):
    return rough_rows(key, 21)


def block_levels(key, shape, shards, low, largest):
    gain = 1.0
    for position, parts in shards:
        heights = jax.random.uniform(jax.random.fold_in(jax.random.fold_in(key, 6), position), (parts,), jnp.float32, low / len(shards), largest / len(shards))
        gain = gain * jnp.repeat(jnp.exp(heights), shape[position] // parts).reshape((-1,) + (1,) * (len(shape) - 1 - position))
    return gain


def shared_out(rng, own, number, rows, count, top, most, skew):
    order = jax.random.permutation(rng, count)
    heavy_load, common = load_shares(count, rows * top, most, skew, True), load_shares(count, rows * top, most, skew, False)
    places = jnp.arange(count)

    def named(sizes, turn):
        used = int((sizes > 0).sum())
        fixed = max(1, used // 4)
        moved = fixed + (places - fixed + turn * (used - fixed)) % max(1, count - fixed)
        return jnp.zeros((count,), jnp.int32).at[order[jnp.where(places < fixed, places, moved)]].set(jnp.asarray(sizes, jnp.int32))

    sizes = jnp.where(number % 4 == 0, named(heavy_load, number // 4), named(common, number - number // 4 - 1))
    mixed = jax.random.permutation(jax.random.fold_in(own, 3), count)
    donor, receiver = mixed[0:count // 2 * 2:2], mixed[1:count // 2 * 2:2]
    room = jnp.minimum(sizes[donor] - 1, most - sizes[receiver]) // 2
    room = jnp.where((donor == order[0]) | (receiver == order[0]) | (sizes[receiver] == 0), 0, jnp.maximum(room, 0))
    moved = jax.random.randint(jax.random.fold_in(own, 4), (count // 2,), 0, 1 << 20) % (room + 1)
    sizes = sizes.at[donor].add(-moved).at[receiver].add(moved)
    items = jnp.searchsorted(jnp.cumsum(sizes), jnp.arange(rows * top), side="right").astype(jnp.int32)
    grid = items.reshape(top, rows).T
    grid = grid[jax.random.permutation(jax.random.fold_in(own, 1), rows)]
    turn = jax.random.randint(jax.random.fold_in(own, 2), (rows, 1), 0, top)
    return jnp.take_along_axis(grid, (jnp.arange(top)[None, :] + turn) % top, axis=1)


def load_shares(amount, total, limit, skew, full):
    portions = [(1 << 20) // math.isqrt(standing ** skew) + 1 for standing in range(1, amount + 1)]
    largest = limit if full else min(limit, max(-(-total // amount), total * portions[0] // sum(portions)))
    least = 1 if total - largest >= amount - 1 else 0
    holding, spare = [largest] + [least] * (amount - 1), total - largest - least * (amount - 1)
    while spare > 0:
        free = [i for i in range(1, amount) if holding[i] < largest] or [i for i in range(1, amount) if holding[i] < limit]
        whole, remaining = sum([portions[i] for i in free]), spare
        for i in free:
            addition = min(limit - holding[i], max(1, remaining * portions[i] // whole), spare)
            holding[i] = holding[i] + addition
            spare = spare - addition
    return np.array(holding)


def bell_draw(rng, extent, deviation, most, split=(), kind=jnp.bfloat16):
    gain = block_levels(rng, extent, split, -0.22, 0.18) if split else 1.0
    drawn = jax.random.normal(rng, extent, jnp.float32) * deviation * gain
    return jnp.minimum(jnp.maximum(drawn, -most), most).astype(kind)


def setup_inputs(seed: int = 0) -> dict:
    arg_keys = jax.random.split(jax.random.key(seed), 7)
    q_in = draw_q_in(jax.random.fold_in(arg_keys[6], 71), 0)
    k_in = draw_k_in(jax.random.fold_in(arg_keys[6], 71), 0)
    v_in = bell_draw(arg_keys[2], (TOKENS, HEADS * HEAD_DIM), 1.0, 6.0, ((0, 256),))
    cotangent = bell_draw(arg_keys[3], (TOKENS, D), 0.3, 1.796875, ((0, 256),))
    out_weight = bell_draw(arg_keys[4], (HEADS * HEAD_DIM, D), (HEADS * HEAD_DIM) ** -0.5, 0.1875)
    cluster_ids_keys = jax.random.split(jax.random.fold_in(arg_keys[5], 1), HEADS * TOKENS // TOK_DEV)
    cluster_ids_turns = jax.random.permutation(jax.random.fold_in(arg_keys[5], 3), HEADS * TOKENS // TOK_DEV)
    cluster_ids = jax.vmap(lambda own, number: shared_out(jax.random.fold_in(arg_keys[5], 2), own, number, TOK_DEV, CLUSTERS, 1, CAP, 2))(cluster_ids_keys, cluster_ids_turns).reshape((HEADS, TOKENS, 1))
    return {"q_in": q_in, "k_in": k_in, "v_in": v_in, "cotangent": cotangent, "out_weight": out_weight, "cluster_ids": cluster_ids}


def one_head(operands):
    query, keys_in, values_in, grad_out, labels = operands
    score_scale = HEAD_DIM ** -0.5
    query_wide = query.astype(jnp.float32)
    keys_wide = keys_in.astype(jnp.float32)
    values_wide = values_in.astype(jnp.float32)
    grad_wide = grad_out.astype(jnp.float32)
    scores = jnp.einsum("id,jd->ij", query_wide, keys_wide) * score_scale
    positions = jnp.arange(LENGTH, dtype=jnp.int32)
    allowed = (labels[:, None] == labels[None, :]) & (positions[None, :] <= positions[:, None])
    scores = jnp.where(allowed, scores, jnp.float32(-1.0e30))
    row_peak = jnp.max(scores, axis=-1, keepdims=True)
    exp_terms = jnp.exp(scores - row_peak)
    weights = exp_terms / jnp.sum(exp_terms, axis=-1, keepdims=True)
    weights_low = weights.astype(jnp.bfloat16).astype(jnp.float32)
    attended = jnp.einsum("ij,jd->id", weights_low, values_wide).astype(jnp.bfloat16)
    grad_prob = jnp.einsum("id,jd->ij", grad_wide, values_wide)
    row_delta = jnp.sum(weights * grad_prob, axis=-1, keepdims=True)
    grad_score = (weights * (grad_prob - row_delta) * score_scale).astype(jnp.bfloat16).astype(jnp.float32)
    query_grad = jnp.einsum("ij,jd->id", grad_score, keys_wide).astype(jnp.bfloat16)
    key_grad = jnp.einsum("ij,id->jd", grad_score, query_wide).astype(jnp.bfloat16)
    value_grad = jnp.einsum("ij,id->jd", weights_low, grad_wide).astype(jnp.bfloat16)
    return attended, query_grad, key_grad, value_grad


def reference(q_in, k_in, v_in, cotangent, out_weight, cluster_ids):
    seq_count = TOKENS // LENGTH
    grad_heads = jnp.dot(cotangent, out_weight.T, preferred_element_type=jnp.float32).astype(jnp.bfloat16)

    def shape_heads(array_in):
        return array_in.reshape(seq_count, LENGTH, HEADS, HEAD_DIM).transpose(0, 2, 1, 3).reshape(seq_count * HEADS, LENGTH, HEAD_DIM)

    def shape_tokens(array_in):
        return array_in.reshape(seq_count, HEADS, LENGTH, HEAD_DIM).transpose(0, 2, 1, 3).reshape(TOKENS, HEADS * HEAD_DIM)

    labels_all = cluster_ids[:, :, 0].reshape(HEADS, seq_count, LENGTH).transpose(1, 0, 2).reshape(seq_count * HEADS, LENGTH)
    attended, query_grad, key_grad, value_grad = lax.map(
        one_head,
        (shape_heads(q_in), shape_heads(k_in), shape_heads(v_in), shape_heads(grad_heads), labels_all))
    attn_out = shape_tokens(attended)
    layer_out = jnp.dot(attn_out, out_weight, preferred_element_type=jnp.float32).astype(jnp.bfloat16)
    wo_grad = jnp.dot(attn_out.T, cotangent, preferred_element_type=jnp.float32) * (TOKENS ** -0.5)
    return (layer_out, shape_tokens(query_grad), shape_tokens(key_grad), shape_tokens(value_grad), wo_grad)
```

```python
import math

import jax
import jax.numpy as jnp
from jax import lax
from jax.experimental import pallas as pl
from jax.experimental.pallas import tpu as pltpu
from jax.sharding import Mesh, PartitionSpec as P

HEADS = 8
HEAD_DIM = 128
CLUSTERS = 64
CAP = 8
TOK = 256
NZ = 8
NX = 4
SLOTS = CLUSTERS * CAP
META = 16
PAIR = 2 * HEAD_DIM
NEG_FILL = -1e30
X_STEP = (0, NX - 1, 1, 2)


def attend_kernel(
    x_ref, own, left, right, opp_lo, opp_hi, qg, attn_o, dq_o, d_own, d_left, d_right, d_opp,
    kvs, qgs, slot_rows, cnts, bias, causal,
):
    half = NZ // 2
    sources = (
        (own, 0, NZ),
        (left, NZ, NZ),
        (right, 2 * NZ, NZ),
        (opp_lo, 3 * NZ, half),
        (opp_hi, 3 * NZ + half, half),
    )
    slot_iota = lax.broadcasted_iota(jnp.int32, (SLOTS, TOK), 0)

    def one_hot(slot_row):
        return jnp.where(slot_iota == slot_row, 1.0, 0.0).astype(jnp.bfloat16)

    for ref, base, count in sources:

        def spread(z, carry, ref=ref, base=base):
            meta = ref[z, TOK : TOK + META, :].astype(jnp.float32)
            slot_row = meta[0:1, :] * CAP + meta[1:2, :]
            slot_rows[pl.ds(base + z, 1), :] = slot_row
            cnts[pl.ds(base + z, 1), :] = meta[2:3, :]
            hot = one_hot(slot_row.astype(jnp.int32))
            rows = jnp.dot(hot, ref[z, 0:TOK, :], preferred_element_type=jnp.float32)
            kvs[:, base + z, :, :] = rows.reshape(CLUSTERS, CAP, PAIR)
            if base == 0:
                rows = jnp.dot(hot, qg[z], preferred_element_type=jnp.float32)
                qgs[:, z, :, :] = rows.reshape(CLUSTERS, CAP, PAIR)
            return carry

        lax.fori_loop(0, count, spread, 0)

    blocks = 4 * NZ
    keys = blocks * CAP
    queries = NZ * CAP
    widen = jnp.where(
        lax.broadcasted_iota(jnp.int32, (blocks, keys), 1) // CAP
        == lax.broadcasted_iota(jnp.int32, (blocks, keys), 0),
        1.0,
        0.0,
    ).astype(jnp.bfloat16)
    held = lax.dot_general(
        cnts[...].astype(jnp.bfloat16), widen, (((0,), (0,)), ((), ())),
        preferred_element_type=jnp.float32,
    )
    lane = lax.broadcasted_iota(jnp.int32, (CLUSTERS, keys), 1) % CAP
    bias[...] = jnp.where(lane.astype(jnp.float32) < held[0:CLUSTERS, :], 0.0, NEG_FILL)

    me = x_ref[0]
    key_at = lax.broadcasted_iota(jnp.int32, (queries, keys), 1)
    source = key_at // (NZ * CAP)
    step = jnp.where(source == 1, X_STEP[1], jnp.where(source == 2, X_STEP[2], jnp.where(source == 3, X_STEP[3], 0)))
    key_x = (me + step) % NX
    key_pos = (((key_at // CAP) % NZ) * NX + key_x) * CAP + key_at % CAP
    query_at = lax.broadcasted_iota(jnp.int32, (queries, keys), 0)
    query_pos = ((query_at // CAP) * NX + me) * CAP + query_at % CAP
    causal[...] = jnp.where(key_pos <= query_pos, 0.0, NEG_FILL)

    score_scale = HEAD_DIM ** (-0.5)
    zeros = jnp.zeros((queries, HEAD_DIM), jnp.bfloat16)

    def attend(c):
        kv = kvs[c].reshape(keys, PAIR).astype(jnp.bfloat16)
        qg_c = qgs[c].reshape(queries, PAIR).astype(jnp.bfloat16)
        diag = jnp.concatenate(
            [
                jnp.concatenate([qg_c[:, :HEAD_DIM], zeros], axis=1),
                jnp.concatenate([zeros, qg_c[:, HEAD_DIM:]], axis=1),
            ],
            axis=0,
        )
        both = lax.dot_general(
            diag, kv, (((1,), (1,)), ((), ())), preferred_element_type=jnp.float32
        )
        scores = both[:queries] * score_scale + (causal[...] + bias[pl.ds(c, 1), :])
        grad_prob = both[queries:]
        peak = jnp.max(scores, axis=-1, keepdims=True)
        terms = jnp.exp(scores - peak)
        weights = terms * (1.0 / jnp.sum(terms, axis=-1, keepdims=True))
        delta = jnp.sum(weights * grad_prob, axis=-1, keepdims=True)
        grad_score = weights * (grad_prob - delta) * score_scale
        low = jnp.concatenate([grad_score.astype(jnp.bfloat16), weights.astype(jnp.bfloat16)], axis=0)
        outs = jnp.dot(low, kv, preferred_element_type=jnp.float32)
        pair = jnp.concatenate([outs[queries:, HEAD_DIM:], outs[:queries, :HEAD_DIM]], axis=1)
        qgs[c] = pair.reshape(NZ, CAP, PAIR)
        key_side = lax.dot_general(
            low, diag, (((0,), (0,)), ((), ())), preferred_element_type=jnp.float32
        )
        kvs[c] = key_side.reshape(blocks, CAP, PAIR)

    group = 4

    def attend_some(step, carry):
        for k in range(group):
            attend(step * group + k)
        return carry

    lax.fori_loop(0, CLUSTERS // group, attend_some, 0)

    lane_iota = lax.broadcasted_iota(jnp.int32, (TOK, HEAD_DIM), 1).astype(jnp.float32)

    def hot_columns(b):
        column = jnp.broadcast_to(slot_rows[pl.ds(b, 1), :], (HEAD_DIM, TOK)).T
        return jnp.concatenate(
            [
                jnp.where(column == lane_iota + float(HEAD_DIM * k), 1.0, 0.0).astype(jnp.bfloat16)
                for k in range(SLOTS // HEAD_DIM)
            ],
            axis=1,
        )

    def collect(hot, slotted):
        rows = slotted.reshape(SLOTS, PAIR).astype(jnp.bfloat16)
        return jnp.dot(hot, rows, preferred_element_type=jnp.float32).astype(jnp.bfloat16)

    for number, ref in enumerate((d_own, d_left, d_right, d_opp)):

        def gather(z, carry, ref=ref, number=number):
            hot = hot_columns(number * NZ + z)
            ref[z] = collect(hot, kvs[:, number * NZ + z, :, :])
            if number == 0:
                got = collect(hot, qgs[:, z, :, :])
                attn_o[z] = got[:, :HEAD_DIM]
                dq_o[z] = got[:, HEAD_DIM:]
            return carry

        lax.fori_loop(0, NZ, gather, 0)


def attend(x_index, own, left, right, opp_lo, opp_hi, qg, interpret=False):
    vmem = pl.BlockSpec(memory_space=pltpu.VMEM)
    bf16 = jnp.bfloat16
    narrow = jax.ShapeDtypeStruct((NZ, TOK, HEAD_DIM), bf16)
    wide = jax.ShapeDtypeStruct((NZ, TOK, PAIR), bf16)
    blocks = 4 * NZ
    return pl.pallas_call(
        attend_kernel,
        out_shape=(narrow, narrow, wide, wide, wide, wide),
        in_specs=[pl.BlockSpec(memory_space=pltpu.SMEM)] + [vmem] * 6,
        out_specs=(vmem,) * 6,
        scratch_shapes=[
            pltpu.VMEM((CLUSTERS, blocks, CAP, PAIR), jnp.float32),
            pltpu.VMEM((CLUSTERS, NZ, CAP, PAIR), jnp.float32),
            pltpu.VMEM((blocks, TOK), jnp.float32),
            pltpu.VMEM((blocks, TOK), jnp.float32),
            pltpu.VMEM((CLUSTERS, blocks * CAP), jnp.float32),
            pltpu.VMEM((NZ * CAP, blocks * CAP), jnp.float32),
        ],
        compiler_params=pltpu.CompilerParams(vmem_limit_bytes=56 * 1024 * 1024),
        cost_estimate=pl.CostEstimate(flops=12 << 30, bytes_accessed=12 << 20, transcendentals=1 << 20),
        interpret=interpret,
    )(x_index, own, left, right, opp_lo, opp_hi, qg)


def shift(value, axis, size, by):
    return lax.ppermute(value, axis, [(i, (i + by) % size) for i in range(size)])


def per_device(q_in, k_in, v_in, cotangent, out_weight, cluster_ids):
    f32, bf16 = jnp.float32, jnp.bfloat16
    ids = cluster_ids[:, :, 0]
    at = jnp.arange(TOK, dtype=jnp.int32)
    same = (ids[:, :, None] == ids[:, None, :]) & (at[:, None] < at[None, :])[None]
    rank = jnp.sum(same.astype(f32), axis=1)
    counts = jnp.sum(
        (ids[:, :, None] == jnp.arange(TOK, dtype=jnp.int32)[None, None, :]).astype(f32), axis=1
    )
    meta = jnp.stack([ids.astype(f32), rank, counts], axis=1)
    meta = jnp.pad(meta, ((0, 0), (0, META - 3), (0, 0))).astype(bf16)

    def by_head(rows):
        return rows.reshape(TOK, HEADS, HEAD_DIM).transpose(1, 0, 2)

    def swap_z(value):
        return lax.all_to_all(value, "z", split_axis=0, concat_axis=0, tiled=True)

    kv = jnp.concatenate(
        [jnp.concatenate([by_head(k_in), by_head(v_in)], axis=2), meta], axis=1
    )
    own = swap_z(kv)
    grad_heads = lax.dot_general(
        cotangent, out_weight, (((1,), (1,)), ((), ())), preferred_element_type=f32
    ).astype(bf16)
    left = shift(own, "x", NX, 1)
    right = shift(own, "x", NX, -1)
    qg = swap_z(jnp.concatenate([by_head(q_in), by_head(grad_heads)], axis=2))
    half = NZ // 2
    opp_lo = shift(left[:half], "x", NX, 1)
    opp_hi = shift(right[half:], "x", NX, -1)
    x_index = lax.axis_index("x").reshape(1).astype(jnp.int32)
    attended, q_part, d_own, d_left, d_right, d_opp = attend(
        x_index, own, left, right, opp_lo, opp_hi, qg
    )

    def from_heads(rows):
        return rows.transpose(1, 0, 2).reshape(TOK, HEADS * HEAD_DIM)

    attn_out = from_heads(swap_z(attended))

    def add(a, b):
        return (a.astype(f32) + b.astype(f32)).astype(bf16)

    far_lo = shift(d_opp[:half], "x", NX, -1)
    far_hi = shift(d_opp[half:], "x", NX, 1)
    near_lo = shift(d_right[:half], "x", NX, 1)
    near_hi = shift(d_left[half:], "x", NX, -1)
    via_lo = shift(add(d_left[:half], far_lo), "x", NX, -1)
    via_hi = shift(add(d_right[half:], far_hi), "x", NX, 1)
    key_side = jnp.concatenate(
        [
            (d_own[:half].astype(f32) + near_lo.astype(f32) + via_lo.astype(f32)).astype(bf16),
            (d_own[half:].astype(f32) + near_hi.astype(f32) + via_hi.astype(f32)).astype(bf16),
        ],
        axis=0,
    )

    width = cotangent.shape[1]
    core = lax.axis_index("core")
    cols = width // 2
    theirs = lax.dynamic_slice_in_dim(cotangent, (1 - core) * cols, cols, axis=1)
    ours = lax.dynamic_slice_in_dim(cotangent, core * cols, cols, axis=1)

    def weight_term(columns):
        return lax.dot_general(
            attn_out, columns, (((0,), (0,)), ((), ())), preferred_element_type=f32
        )

    other = shift(weight_term(theirs).astype(bf16), "core", 2, 1)
    term = weight_term(ours) + other.astype(f32)
    rows = HEADS * HEAD_DIM
    parts = term.astype(bf16).reshape(rows, 4, cols // 4).transpose(1, 0, 2)
    parts = lax.all_to_all(parts, "y", split_axis=0, concat_axis=0, tiled=True)
    term = jnp.sum(parts.astype(f32), axis=0)
    parts = term.astype(bf16).reshape(NZ * NX, rows // (NZ * NX), cols // 4)
    parts = lax.all_to_all(parts, ("z", "x"), split_axis=0, concat_axis=0, tiled=True)
    grad_factor = 1.0 / math.sqrt(TOK * NZ * NX * 8)
    term = jnp.sum(parts.astype(f32), axis=0) * grad_factor
    spread = jnp.broadcast_to(term[None], (8,) + term.shape)
    blocks = lax.all_to_all(spread, ("core", "y"), split_axis=0, concat_axis=0, tiled=True)
    wo_grad = blocks.transpose(1, 0, 2).reshape(rows // (NZ * NX), width)

    layer_out = jnp.dot(attn_out, out_weight, preferred_element_type=f32).astype(bf16)
    q_grad = from_heads(swap_z(q_part))
    kv_grad = swap_z(key_side)
    k_grad = from_heads(kv_grad[:, :, :HEAD_DIM])
    v_grad = from_heads(kv_grad[:, :, HEAD_DIM:])
    return (layer_out, q_grad, k_grad, v_grad, wo_grad)


def solution(mesh):
    mesh = Mesh(mesh.devices.reshape(4, 2, NZ, NX), ("y", "core", "z", "x"))
    tokens = ("y", "core", "z", "x")
    placed = (
        P(tokens, None),
        P(tokens, None),
        P(tokens, None),
        P(tokens, None),
        P(),
        P(None, tokens, None),
    )
    return jax.shard_map(
        per_device,
        mesh=mesh,
        in_specs=placed,
        out_specs=(
            P(tokens, None),
            P(tokens, None),
            P(tokens, None),
            P(tokens, None),
            P(("z", "x"), None),
        ),
        check_vma=False,
    )
```

```python
import functools
import math

import jax
import jax.numpy as jnp
from jax import lax
from jax.experimental import pallas as pl
from jax.experimental.pallas import tpu as pltpu
from jax.sharding import Mesh, PartitionSpec as P

HEADS = 8
HEAD_DIM = 128
CLUSTERS = 64
CAP = 8
TOK = 256
NZ = 8
NX = 4
SLOTS = CLUSTERS * CAP
META = 16
GROUP = 4
PAIR = 2 * HEAD_DIM
NEG_FILL = -1e30
X_STEP = (0, NX - 1, 1, 2)


def slot_row_of(meta):
    ids = jnp.concatenate([meta[0:1, :], meta[1:2, :]], axis=1)
    rank = jnp.concatenate([meta[2:3, :], meta[3:4, :]], axis=1)
    return ids * CAP + rank


def spread_rows(meta, rows):
    slot_iota = lax.broadcasted_iota(jnp.int32, (SLOTS, TOK), 0)
    hot = jnp.where(slot_iota == slot_row_of(meta).astype(jnp.int32), 1.0, 0.0).astype(jnp.bfloat16)
    out = jnp.dot(hot, rows, preferred_element_type=jnp.float32)
    return out.reshape(CLUSTERS, CAP, PAIR)


def spread_keys_kernel(base, key_in, value_in, slots, held, counts):
    pairs = key_in.shape[0] // 2

    def some(z2, carry):
        got = []
        for i in range(2):
            z = 2 * z2 + i
            meta = key_in[z, TOK : TOK + META, :].astype(jnp.float32)
            counts[pl.ds(z, 1), :] = meta[4:5, :]
            rows = jnp.concatenate([key_in[z, 0:TOK, :], value_in[z]], axis=1)
            got.append(spread_rows(meta, rows))
        slots[:, z2] = jnp.concatenate(got, axis=1).astype(jnp.bfloat16)
        return carry

    lax.fori_loop(0, pairs, some, 0)
    keys = 4 * NZ * CAP
    number = 2 * pairs
    widen = jnp.where(
        lax.broadcasted_iota(jnp.int32, (number, keys), 1) // CAP
        == lax.broadcasted_iota(jnp.int32, (number, keys), 0) + base,
        1.0,
        0.0,
    )
    wide = lax.dot_general(
        counts[...], widen, (((0,), (0,)), ((), ())), preferred_element_type=jnp.float32
    )
    held[...] = wide[0:CLUSTERS, :]


def spread_queries_kernel(meta_in, qg, slots):
    def some(z2, carry):
        got = [
            spread_rows(meta_in[2 * z2 + i].astype(jnp.float32), qg[2 * z2 + i]) for i in range(2)
        ]
        slots[:, z2] = jnp.concatenate(got, axis=1).astype(jnp.bfloat16)
        return carry

    lax.fori_loop(0, NZ // 2, some, 0)


def attend_kernel(
    x_ref, own, left, right, opp_lo, opp_hi, qg, held_0, held_1, held_2, held_3, held_4,
    aq, d_own, d_left, d_right, d_opp_lo, d_opp_hi, bias, causal,
):
    keys = 4 * NZ * CAP
    queries = NZ * CAP

    @pl.when(pl.program_id(0) == 0)
    def _():
        held = held_0[...] + held_1[...] + held_2[...] + held_3[...] + held_4[...]
        lane = lax.broadcasted_iota(jnp.int32, (CLUSTERS, keys), 1) % CAP
        bias[...] = jnp.where(lane.astype(jnp.float32) < held, 0.0, NEG_FILL)
        me = x_ref[0]
        key_at = lax.broadcasted_iota(jnp.int32, (queries, keys), 1)
        source = key_at // (NZ * CAP)
        step = jnp.where(
            source == 1,
            X_STEP[1],
            jnp.where(source == 2, X_STEP[2], jnp.where(source == 3, X_STEP[3], 0)),
        )
        key_x = (me + step) % NX
        key_pos = (((key_at // CAP) % NZ) * NX + key_x) * CAP + key_at % CAP
        query_at = lax.broadcasted_iota(jnp.int32, (queries, keys), 0)
        query_pos = ((query_at // CAP) * NX + me) * CAP + query_at % CAP
        causal[...] = jnp.where(key_pos <= query_pos, 0.0, NEG_FILL)

    score_scale = HEAD_DIM ** (-0.5)
    zeros = jnp.zeros((queries, HEAD_DIM), jnp.bfloat16)
    first = pl.program_id(0) * GROUP
    many = range(GROUP)
    parts = (own, left, right, opp_lo, opp_hi)
    kv = [
        jnp.concatenate([part[k].reshape(part.shape[1] * 2 * CAP, PAIR) for part in parts], axis=0)
        for k in many
    ]
    diag = []
    for k in many:
        qg_k = qg[k].reshape(queries, PAIR)
        diag.append(
            jnp.concatenate(
                [
                    jnp.concatenate([qg_k[:, :HEAD_DIM], zeros], axis=1),
                    jnp.concatenate([zeros, qg_k[:, HEAD_DIM:]], axis=1),
                ],
                axis=0,
            )
        )
    both = [
        lax.dot_general(
            diag[k], kv[k], (((1,), (1,)), ((), ())), preferred_element_type=jnp.float32
        )
        for k in many
    ]
    low = []
    for k in many:
        scores = both[k][:queries] * score_scale + (causal[...] + bias[pl.ds(first + k, 1), :])
        grad_prob = both[k][queries:]
        peak = jnp.max(scores, axis=-1, keepdims=True)
        terms = jnp.exp(scores - peak)
        weights = terms * (1.0 / jnp.sum(terms, axis=-1, keepdims=True))
        delta = jnp.sum(weights * grad_prob, axis=-1, keepdims=True)
        grad_score = weights * (grad_prob - delta) * score_scale
        low.append(
            jnp.concatenate(
                [grad_score.astype(jnp.bfloat16), weights.astype(jnp.bfloat16)], axis=0
            )
        )
    outs = [jnp.dot(low[k], kv[k], preferred_element_type=jnp.float32) for k in many]
    key_side = [
        lax.dot_general(
            low[k], diag[k], (((0,), (0,)), ((), ())), preferred_element_type=jnp.float32
        ).astype(jnp.bfloat16)
        for k in many
    ]
    for k in many:
        pair = jnp.concatenate([outs[k][queries:, HEAD_DIM:], outs[k][:queries, :HEAD_DIM]], axis=1)
        aq[k] = pair.astype(jnp.bfloat16).reshape(NZ // 2, 2 * CAP, PAIR)
        at = 0
        for ref in (d_own, d_left, d_right, d_opp_lo, d_opp_hi):
            size = ref.shape[1] * 2 * CAP
            ref[k] = key_side[k][at : at + size].reshape(ref.shape[1], 2 * CAP, PAIR)
            at += size


def gather_kernel(split, meta_in, slots, *outs):
    lane_iota = lax.broadcasted_iota(jnp.int32, (TOK, HEAD_DIM), 1).astype(jnp.float32)

    def hot_columns(z):
        slot_row = slot_row_of(meta_in[z].astype(jnp.float32))
        column = jnp.broadcast_to(slot_row, (HEAD_DIM, TOK)).T
        return jnp.concatenate(
            [
                jnp.where(column == lane_iota + float(HEAD_DIM * k), 1.0, 0.0).astype(jnp.bfloat16)
                for k in range(SLOTS // HEAD_DIM)
            ],
            axis=1,
        )

    def some(z2, write):
        wide = slots[:, z2].astype(jnp.float32)
        for i in range(2):
            rows = wide[:, i * CAP : (i + 1) * CAP, :].reshape(SLOTS, PAIR).astype(jnp.bfloat16)
            got = jnp.dot(hot_columns(2 * z2 + i), rows, preferred_element_type=jnp.float32)
            write(2 * z2 + i, got.astype(jnp.bfloat16))

    if split:

        def halves(z, got):
            outs[0][z] = got[:, :HEAD_DIM]
            outs[1][z] = got[:, HEAD_DIM:]

        def step(z2, carry):
            some(z2, halves)
            return carry

        lax.fori_loop(0, slots.shape[1], step, 0)
        return
    for number, out in enumerate(outs):
        pairs = out.shape[0] // 2

        def step(z2, carry, out=out, base=number * pairs):
            def write(z, got):
                out[z - 2 * base] = got

            some(base + z2, write)
            return carry

        lax.fori_loop(0, pairs, step, 0)


VMEM = pl.BlockSpec(memory_space=pltpu.VMEM)
BF16 = jnp.bfloat16


def cost(flops, size):
    return pl.CostEstimate(flops=flops, bytes_accessed=size, transcendentals=0)


def spread_keys(base, key_in, value_in):
    count = key_in.shape[0]
    return pl.pallas_call(
        functools.partial(spread_keys_kernel, base),
        out_shape=(
            jax.ShapeDtypeStruct((CLUSTERS, count // 2, 2 * CAP, PAIR), BF16),
            jax.ShapeDtypeStruct((CLUSTERS, 4 * NZ * CAP), jnp.float32),
        ),
        in_specs=[VMEM, VMEM],
        out_specs=(VMEM, VMEM),
        scratch_shapes=[pltpu.VMEM((count, HEAD_DIM), jnp.float32)],
        cost_estimate=cost(count << 26, count << 18),
        name="spread_keys",
    )(key_in, value_in)


def meta_spec(count):
    return pl.BlockSpec((count, META, HEAD_DIM), lambda i: (0, TOK // META, 0))


def whole(shape):
    return pl.BlockSpec(shape, lambda i: (0,) * len(shape))


def spread_queries(key_in, qg):
    shape = (CLUSTERS, NZ // 2, 2 * CAP, PAIR)
    return pl.pallas_call(
        spread_queries_kernel,
        grid=(1,),
        out_shape=jax.ShapeDtypeStruct(shape, BF16),
        in_specs=[meta_spec(NZ), whole(qg.shape)],
        out_specs=whole(shape),
        cost_estimate=cost(NZ << 26, NZ << 18),
        name="spread_queries",
    )(key_in, qg)


def attend(x_index, slots, held, qg):
    def part(shape):
        return pl.BlockSpec((GROUP,) + shape[1:], lambda i: (i, 0, 0, 0))

    keys = 4 * NZ * CAP
    shapes = [qg.shape] + [s.shape for s in slots]
    return pl.pallas_call(
        attend_kernel,
        grid=(CLUSTERS // GROUP,),
        out_shape=[jax.ShapeDtypeStruct(s, BF16) for s in shapes],
        in_specs=[pl.BlockSpec(memory_space=pltpu.SMEM)]
        + [part(s.shape) for s in slots]
        + [part(qg.shape)]
        + [whole((CLUSTERS, keys))] * len(held),
        out_specs=[part(s) for s in shapes],
        scratch_shapes=[
            pltpu.VMEM((CLUSTERS, keys), jnp.float32),
            pltpu.VMEM((NZ * CAP, keys), jnp.float32),
        ],
        cost_estimate=cost(8 << 30, 20 << 20),
        name="attend",
    )(x_index, *slots, qg, *held)


def gather(split, key_in, slots):
    count = key_in.shape[0]
    if split:
        shapes = [(count, TOK, HEAD_DIM)] * 2
    else:
        shapes = [(NZ // 2, TOK, PAIR)] * (count // (NZ // 2))
    return pl.pallas_call(
        functools.partial(gather_kernel, split),
        grid=(1,),
        out_shape=[jax.ShapeDtypeStruct(s, BF16) for s in shapes],
        in_specs=[meta_spec(count), whole(slots.shape)],
        out_specs=[whole(s) for s in shapes],
        cost_estimate=cost(count << 26, count << 18),
        name="gather_rows",
    )(key_in, slots)


def shift(value, axis, size, by):
    return lax.ppermute(value, axis, [(i, (i + by) % size) for i in range(size)])


def meta_rows(cluster_ids):
    f32 = jnp.float32
    ids = cluster_ids[:, :, 0]
    at = jnp.arange(TOK, dtype=jnp.int32)
    same = (ids[:, :, None] == ids[:, None, :]) & (at[:, None] < at[None, :])[None]
    rank = jnp.sum(same.astype(f32), axis=1)
    counts = jnp.sum(
        (ids[:, :, None] == jnp.arange(HEAD_DIM, dtype=jnp.int32)[None, None, :]).astype(f32), axis=1
    )
    rows = jnp.concatenate(
        [
            ids.astype(f32).reshape(HEADS, 2, HEAD_DIM),
            rank.reshape(HEADS, 2, HEAD_DIM),
            counts.reshape(HEADS, 1, HEAD_DIM),
        ],
        axis=1,
    )
    return jnp.pad(rows, ((0, 0), (0, META - 5), (0, 0))).astype(BF16)


def per_device(q_in, k_in, v_in, cotangent, out_weight, cluster_ids):
    f32, bf16 = jnp.float32, BF16
    half = NZ // 2

    def by_head(rows):
        return rows.reshape(TOK, HEADS, HEAD_DIM).transpose(1, 0, 2)

    def swap_z(value):
        return lax.all_to_all(value, "z", split_axis=0, concat_axis=0, tiled=True)

    def column(value):
        left = shift(value, "x", NX, 1)
        right = shift(value, "x", NX, -1)
        return (
            value, left, right, shift(left[:half], "x", NX, 1), shift(right[half:], "x", NX, -1)
        )

    keys = column(swap_z(jnp.concatenate([by_head(k_in), meta_rows(cluster_ids)], axis=1)))
    values = column(swap_z(by_head(v_in)))
    grad_heads = lax.dot_general(
        cotangent, out_weight, (((1,), (1,)), ((), ())), preferred_element_type=f32
    ).astype(bf16)
    qg = swap_z(jnp.concatenate([by_head(q_in), by_head(grad_heads)], axis=2))
    bases = (0, NZ, 2 * NZ, 3 * NZ, 3 * NZ + half)
    spread = [spread_keys(b, k, v) for b, k, v in zip(bases, keys, values)]
    qg_slots = spread_queries(keys[0], qg)
    x_index = lax.axis_index("x").reshape(1).astype(jnp.int32)
    aq, *d_slots = attend(x_index, [s[0] for s in spread], [s[1] for s in spread], qg_slots)

    def from_heads(rows):
        return rows.transpose(1, 0, 2).reshape(TOK, HEADS * HEAD_DIM)

    def add(*terms):
        total = terms[0].astype(f32)
        for term in terms[1:]:
            total = total + term.astype(f32)
        return total.astype(bf16)

    def ring_sum(own, left, right, opp, axis, guard):
        far_lo = shift(opp[0], axis, 4, -1)
        far_hi = shift(opp[1], axis, 4, 1)
        near_lo = shift(right[0], axis, 4, 1)
        near_hi = shift(left[1], axis, 4, -1)
        far_lo, far_hi, near_lo, near_hi, guard = lax.optimization_barrier(
            (far_lo, far_hi, near_lo, near_hi, guard)
        )
        via_lo = shift(add(left[0], far_lo), axis, 4, -1)
        via_hi = shift(add(right[1], far_hi), axis, 4, 1)
        return add(own[0], near_lo, via_lo), add(own[1], near_hi, via_hi), guard

    attended, q_part = gather(True, keys[0], aq)
    attn_heads = swap_z(attended)
    sums = [gather(False, k, d) for k, d in zip(keys, d_slots)]
    opp = (sums[3][0], sums[4][0])
    key_lo, key_hi, attn_heads = ring_sum(sums[0], sums[1], sums[2], opp, "x", attn_heads)
    attn_out = from_heads(attn_heads)

    y, core = lax.axis_index("y"), lax.axis_index("core")
    width = cotangent.shape[1]
    piece = width // 8

    def columns(which):
        return jnp.concatenate(
            [
                lax.dynamic_slice_in_dim(
                    cotangent, which * (4 * piece) + ((y + r) % 4) * piece, piece, axis=1
                )
                for r in range(4)
            ],
            axis=1,
        )

    def weight_term(these):
        return lax.dot_general(
            attn_out, these, (((0,), (0,)), ((), ())), preferred_element_type=f32
        )

    other = shift(weight_term(columns(1 - core)).astype(bf16), "core", 2, 1)
    term = (weight_term(columns(core)) + other.astype(f32)).astype(bf16)
    rows = HEADS * HEAD_DIM

    def block(r):
        here = term[:, r * piece : (r + 1) * piece]
        return here[: rows // 2], here[rows // 2 :]

    q_heads = swap_z(q_part)
    key_lo, key_hi, q_heads = lax.optimization_barrier((key_lo, key_hi, q_heads))
    kv_heads = swap_z(jnp.concatenate([key_lo, key_hi], axis=0))
    term_lo, term_hi, _ = ring_sum(block(0), block(3), block(1), block(2), "y", x_index)
    term_lo, term_hi, kv_heads = lax.optimization_barrier((term_lo, term_hi, kv_heads))
    parts = jnp.concatenate([term_lo, term_hi], axis=0).reshape(NZ * NX, rows // (NZ * NX), piece)
    parts = lax.all_to_all(parts, ("z", "x"), split_axis=0, concat_axis=0, tiled=True)
    grad_factor = 1.0 / math.sqrt(TOK * NZ * NX * 8)
    mine = jnp.sum(parts.astype(f32), axis=0) * grad_factor
    mine = jnp.broadcast_to(mine[None], (8,) + mine.shape)
    blocks = lax.all_to_all(mine, ("core", "y"), split_axis=0, concat_axis=0, tiled=True)
    wo_grad = blocks.transpose(1, 0, 2).reshape(rows // (NZ * NX), width)

    layer_out = jnp.dot(attn_out, out_weight, preferred_element_type=f32).astype(bf16)
    q_grad = from_heads(q_heads)
    k_grad = from_heads(kv_heads[:, :, :HEAD_DIM])
    v_grad = from_heads(kv_heads[:, :, HEAD_DIM:])
    return (layer_out, q_grad, k_grad, v_grad, wo_grad)


def solution(mesh):
    mesh = Mesh(mesh.devices.reshape(4, 2, NZ, NX), ("y", "core", "z", "x"))
    tokens = ("y", "core", "z", "x")
    placed = (
        P(tokens, None),
        P(tokens, None),
        P(tokens, None),
        P(tokens, None),
        P(),
        P(None, tokens, None),
    )
    return jax.shard_map(
        per_device,
        mesh=mesh,
        in_specs=placed,
        out_specs=(
            P(tokens, None),
            P(tokens, None),
            P(tokens, None),
            P(tokens, None),
            P(("z", "x"), None),
        ),
        check_vma=False,
    )
```

```python
import functools
import math

import jax
import jax.numpy as jnp
from jax import lax
from jax.experimental import pallas as pl
from jax.experimental.pallas import tpu as pltpu
from jax.sharding import Mesh, PartitionSpec as P


HEADS = 8
HEAD_DIM = 128
CLUSTERS = 64
CAP = 8
TOK = 256
NZ = 8
NX = 4
SLOTS = CLUSTERS * CAP
META = 16
GROUP = 4
PAIR = 2 * HEAD_DIM
NEG_FILL = -1e30
X_STEP = (0, NX - 1, 1, 2)


def slot_row_of(meta):
    return meta[0:1, :] * CAP + meta[1:2, :]


def spread_rows(meta, rows):
    slot_iota = lax.broadcasted_iota(jnp.int32, (SLOTS, TOK), 0)
    hot = jnp.where(slot_iota == slot_row_of(meta).astype(jnp.int32), 1.0, 0.0).astype(jnp.bfloat16)
    out = jnp.dot(hot, rows, preferred_element_type=jnp.float32)
    return out.reshape(CLUSTERS, CAP, PAIR)


def spread_keys_kernel(base, *refs):
    *ins, slots, held, counts = refs
    for number, ref in enumerate(ins):
        pairs = ref.shape[0] // 2

        def some(z2, carry, ref=ref, first=number * pairs):
            got = []
            for i in range(2):
                z = 2 * z2 + i
                meta = ref[z, TOK : TOK + META, :].astype(jnp.float32)
                counts[pl.ds(2 * first + z, 1), :] = meta[2:3, :]
                got.append(spread_rows(meta, ref[z, 0:TOK, :]))
            slots[:, first + z2] = jnp.concatenate(got, axis=1).astype(jnp.bfloat16)
            return carry

        lax.fori_loop(0, pairs, some, 0)
    keys = 4 * NZ * CAP
    widen = jnp.where(
        lax.broadcasted_iota(jnp.int32, (NZ, keys), 1) // CAP
        == lax.broadcasted_iota(jnp.int32, (NZ, keys), 0) + base,
        1.0,
        0.0,
    )
    wide = lax.dot_general(
        counts[...], widen, (((0,), (0,)), ((), ())), preferred_element_type=jnp.float32
    )
    held[...] = wide[0:CLUSTERS, :]


def spread_queries_kernel(meta_lo, meta_hi, qg, slots):
    half = NZ // 4
    for ref, first in ((meta_lo, 0), (meta_hi, half)):

        def some(z2, carry, ref=ref, first=first):
            got = [
                spread_rows(ref[2 * z2 + i].astype(jnp.float32), qg[2 * (first + z2) + i])
                for i in range(2)
            ]
            slots[:, first + z2] = jnp.concatenate(got, axis=1).astype(jnp.bfloat16)
            return carry

        lax.fori_loop(0, half, some, 0)


def attend_kernel(
    x_ref, own, left, right, opp, qg, held_0, held_1, held_2, held_3,
    aq, d_own, d_left, d_right, d_opp, bias, causal,
):
    keys = 4 * NZ * CAP
    queries = NZ * CAP

    @pl.when(pl.program_id(0) == 0)
    def _():
        held = held_0[...] + held_1[...] + held_2[...] + held_3[...]
        lane = lax.broadcasted_iota(jnp.int32, (CLUSTERS, keys), 1) % CAP
        bias[...] = jnp.where(lane.astype(jnp.float32) < held, 0.0, NEG_FILL)
        me = x_ref[0]
        key_at = lax.broadcasted_iota(jnp.int32, (queries, keys), 1)
        source = key_at // (NZ * CAP)
        step = jnp.where(
            source == 1,
            X_STEP[1],
            jnp.where(source == 2, X_STEP[2], jnp.where(source == 3, X_STEP[3], 0)),
        )
        key_x = (me + step) % NX
        key_pos = (((key_at // CAP) % NZ) * NX + key_x) * CAP + key_at % CAP
        query_at = lax.broadcasted_iota(jnp.int32, (queries, keys), 0)
        query_pos = ((query_at // CAP) * NX + me) * CAP + query_at % CAP
        causal[...] = jnp.where(key_pos <= query_pos, 0.0, NEG_FILL)

    score_scale = HEAD_DIM ** (-0.5)
    zeros = jnp.zeros((queries, HEAD_DIM), jnp.bfloat16)
    first = pl.program_id(0) * GROUP
    many = range(GROUP)
    parts = (own, left, right, opp)
    kv = [
        jnp.concatenate([part[k].reshape(part.shape[1] * 2 * CAP, PAIR) for part in parts], axis=0)
        for k in many
    ]
    diag = []
    for k in many:
        qg_k = qg[k].reshape(queries, PAIR)
        diag.append(
            jnp.concatenate(
                [
                    jnp.concatenate([qg_k[:, :HEAD_DIM], zeros], axis=1),
                    jnp.concatenate([zeros, qg_k[:, HEAD_DIM:]], axis=1),
                ],
                axis=0,
            )
        )
    both = [
        lax.dot_general(
            diag[k], kv[k], (((1,), (1,)), ((), ())), preferred_element_type=jnp.float32
        )
        for k in many
    ]
    low = []
    for k in many:
        scores = both[k][:queries] * score_scale + (causal[...] + bias[pl.ds(first + k, 1), :])
        grad_prob = both[k][queries:]
        peak = jnp.max(scores, axis=-1, keepdims=True)
        terms = jnp.exp(scores - peak)
        weights = terms * (1.0 / jnp.sum(terms, axis=-1, keepdims=True))
        delta = jnp.sum(weights * grad_prob, axis=-1, keepdims=True)
        grad_score = weights * (grad_prob - delta) * score_scale
        low.append(
            jnp.concatenate(
                [grad_score.astype(jnp.bfloat16), weights.astype(jnp.bfloat16)], axis=0
            )
        )
    outs = [jnp.dot(low[k], kv[k], preferred_element_type=jnp.float32) for k in many]
    key_side = [
        lax.dot_general(
            low[k], diag[k], (((0,), (0,)), ((), ())), preferred_element_type=jnp.float32
        ).astype(jnp.bfloat16)
        for k in many
    ]
    for k in many:
        pair = jnp.concatenate([outs[k][queries:, HEAD_DIM:], outs[k][:queries, :HEAD_DIM]], axis=1)
        aq[k] = pair.astype(jnp.bfloat16).reshape(NZ // 2, 2 * CAP, PAIR)
        at = 0
        for ref in (d_own, d_left, d_right, d_opp):
            size = ref.shape[1] * 2 * CAP
            ref[k] = key_side[k][at : at + size].reshape(ref.shape[1], 2 * CAP, PAIR)
            at += size


def gather_kernel(halves, meta_lo, meta_hi, slots, *outs):
    lane_iota = lax.broadcasted_iota(jnp.int32, (TOK, HEAD_DIM), 1).astype(jnp.float32)
    half = NZ // 4

    def hot_columns(meta):
        column = jnp.broadcast_to(slot_row_of(meta.astype(jnp.float32)), (HEAD_DIM, TOK)).T
        return jnp.concatenate(
            [
                jnp.where(column == lane_iota + float(HEAD_DIM * k), 1.0, 0.0).astype(jnp.bfloat16)
                for k in range(SLOTS // HEAD_DIM)
            ],
            axis=1,
        )

    for number, meta_in in enumerate((meta_lo, meta_hi)):
        base = number * half

        def step(z2, carry, out=outs[number], base=base, meta_in=meta_in):
            wide = slots[:, base + z2].astype(jnp.float32)
            for i in range(2):
                rows = wide[:, i * CAP : (i + 1) * CAP, :].reshape(SLOTS, PAIR)
                got = jnp.dot(
                    hot_columns(meta_in[2 * z2 + i]),
                    rows.astype(jnp.bfloat16),
                    preferred_element_type=jnp.float32,
                )
                got = got.astype(jnp.bfloat16)
                if halves:
                    out[2 * z2 + i] = got
                else:
                    outs[0][2 * (base + z2) + i] = got[:, :HEAD_DIM]
                    outs[1][2 * (base + z2) + i] = got[:, HEAD_DIM:]
            return carry

        lax.fori_loop(0, half, step, 0)


VMEM = pl.BlockSpec(memory_space=pltpu.VMEM)
BF16 = jnp.bfloat16


def cost(flops, size):
    return pl.CostEstimate(flops=flops, bytes_accessed=size, transcendentals=0)


def spread_keys(base, lo, hi):
    ins = (lo, hi)
    return pl.pallas_call(
        functools.partial(spread_keys_kernel, base),
        out_shape=(
            jax.ShapeDtypeStruct((CLUSTERS, NZ // 2, 2 * CAP, PAIR), BF16),
            jax.ShapeDtypeStruct((CLUSTERS, 4 * NZ * CAP), jnp.float32),
        ),
        in_specs=[VMEM] * len(ins),
        out_specs=(VMEM, VMEM),
        scratch_shapes=[pltpu.VMEM((NZ, TOK), jnp.float32)],
        cost_estimate=cost(NZ << 26, NZ << 18),
        name="spread_keys",
    )(*ins)


def meta_spec():
    return pl.BlockSpec((NZ // 2, META, PAIR), lambda i: (0, TOK // META, 0))


def whole(shape):
    return pl.BlockSpec(shape, lambda i: (0,) * len(shape))


def spread_queries(lo, hi, qg):
    shape = (CLUSTERS, NZ // 2, 2 * CAP, PAIR)
    return pl.pallas_call(
        spread_queries_kernel,
        grid=(1,),
        out_shape=jax.ShapeDtypeStruct(shape, BF16),
        in_specs=[meta_spec(), meta_spec(), whole(qg.shape)],
        out_specs=whole(shape),
        cost_estimate=cost(NZ << 26, NZ << 18),
        name="spread_queries",
    )(lo, hi, qg)


def attend(x_index, slots, held, qg):
    def part(shape):
        return pl.BlockSpec((GROUP,) + shape[1:], lambda i: (i, 0, 0, 0))

    keys = 4 * NZ * CAP
    shapes = [qg.shape] + [s.shape for s in slots]
    return pl.pallas_call(
        attend_kernel,
        grid=(CLUSTERS // GROUP,),
        out_shape=[jax.ShapeDtypeStruct(s, BF16) for s in shapes],
        in_specs=[pl.BlockSpec(memory_space=pltpu.SMEM)]
        + [part(s.shape) for s in slots]
        + [part(qg.shape)]
        + [whole((CLUSTERS, keys))] * len(held),
        out_specs=[part(s) for s in shapes],
        scratch_shapes=[
            pltpu.VMEM((CLUSTERS, keys), jnp.float32),
            pltpu.VMEM((NZ * CAP, keys), jnp.float32),
        ],
        cost_estimate=cost(8 << 30, 20 << 20),
        name="attend",
    )(x_index, *slots, qg, *held)


def gather(pair, slots, halves):
    shapes = [(NZ // 2, TOK, PAIR) if halves else (NZ, TOK, HEAD_DIM)] * 2
    return pl.pallas_call(
        functools.partial(gather_kernel, halves),
        grid=(1,),
        out_shape=[jax.ShapeDtypeStruct(s, BF16) for s in shapes],
        in_specs=[meta_spec(), meta_spec(), whole(slots.shape)],
        out_specs=[whole(s) for s in shapes],
        cost_estimate=cost(NZ << 26, NZ << 18),
        name="gather_rows",
    )(*pair, slots)


def shift(value, axis, size, by):
    return lax.ppermute(value, axis, [(i, (i + by) % size) for i in range(size)])


def meta_rows(cluster_ids):
    f32 = jnp.float32
    ids = cluster_ids[:, :, 0]
    at = jnp.arange(TOK, dtype=jnp.int32)
    same = (ids[:, :, None] == ids[:, None, :]) & (at[:, None] < at[None, :])[None]
    rank = jnp.sum(same.astype(f32), axis=1)
    counts = jnp.sum((ids[:, :, None] == at[None, None, :]).astype(f32), axis=1)
    rows = jnp.stack([ids.astype(f32), rank, counts], axis=1)
    return jnp.pad(rows, ((0, 0), (0, META - 3), (0, 0))).astype(BF16)


def add(*terms):
    total = terms[0].astype(jnp.float32)
    for term in terms[1:]:
        total = total + term.astype(jnp.float32)
    return total.astype(BF16)


def layer(q_in, k_in, v_in, cotangent, out_weight, cluster_ids):
    f32, bf16 = jnp.float32, BF16
    half = NZ // 2

    def by_head(rows):
        return rows.reshape(TOK, HEADS, HEAD_DIM).transpose(1, 0, 2)

    def from_heads(rows):
        return rows.transpose(1, 0, 2).reshape(TOK, HEADS * HEAD_DIM)

    def swap_z(value):
        return lax.all_to_all(value, "z", split_axis=0, concat_axis=0, tiled=True)

    kv = jnp.concatenate(
        [jnp.concatenate([by_head(k_in), by_head(v_in)], axis=2), meta_rows(cluster_ids)], axis=1
    )
    kv = swap_z(kv)
    own = (kv[:half], kv[half:])
    left_lo = shift(own[0], "x", NX, 1)
    right_hi = shift(own[1], "x", NX, -1)
    left = (left_lo, shift(own[1], "x", NX, 1))
    right = (shift(own[0], "x", NX, -1), right_hi)
    opp = (shift(left_lo, "x", NX, 1), shift(right_hi, "x", NX, -1))
    grad_heads = lax.dot_general(
        cotangent, out_weight, (((1,), (1,)), ((), ())), preferred_element_type=f32
    ).astype(bf16)
    qg = swap_z(jnp.concatenate([by_head(q_in), by_head(grad_heads)], axis=2))
    columns = (own, left, right, opp)
    spread = []
    for number, pair in enumerate(columns):
        spread.append(spread_keys(number * NZ, *pair))
    qg_slots = spread_queries(*own, qg)
    x_index = lax.axis_index("x").reshape(1).astype(jnp.int32)
    aq, *d_slots = attend(x_index, [t[0] for t in spread], [t[1] for t in spread], qg_slots)

    attn_rows, q_rows = gather(own, aq, False)
    attn_out = from_heads(swap_z(attn_rows))
    q_grad = from_heads(swap_z(q_rows))
    sums = []
    for number, pair in enumerate(columns):
        sums.append(gather(pair, d_slots[number], True))
    own_d, left_d, right_d, opp_d = sums
    far_lo = shift(opp_d[0], "x", NX, -1)
    far_hi = shift(opp_d[1], "x", NX, 1)
    near_hi = shift(left_d[1], "x", NX, -1)
    near_lo = shift(right_d[0], "x", NX, 1)
    via_lo = shift(add(left_d[0], far_lo), "x", NX, -1)
    via_hi = shift(add(right_d[1], far_hi), "x", NX, 1)
    key_side = jnp.concatenate(
        [add(own_d[0], near_lo, via_lo), add(own_d[1], near_hi, via_hi)], axis=0
    )
    kv_heads = swap_z(key_side)

    y, core = lax.axis_index("y"), lax.axis_index("core")
    width = cotangent.shape[1]
    piece = width // 8
    rows = HEADS * HEAD_DIM

    def column_blocks(which):
        return jnp.concatenate(
            [
                lax.dynamic_slice_in_dim(
                    cotangent, which * (4 * piece) + ((y + r) % 4) * piece, piece, axis=1
                )
                for r in range(4)
            ],
            axis=1,
        )

    def weight_term(these):
        return lax.dot_general(
            attn_out, these, (((0,), (0,)), ((), ())), preferred_element_type=f32
        )

    other = shift(weight_term(column_blocks(1 - core)).astype(bf16), "core", 2, 1)
    term = (weight_term(column_blocks(core)) + other.astype(f32)).astype(bf16)

    def block(r, upper):
        here = term[:, r * piece : (r + 1) * piece]
        return here[rows // 2 :] if upper else here[: rows // 2]

    far_lo = shift(block(2, False), "y", 4, -1)
    far_hi = shift(block(2, True), "y", 4, 1)
    near_hi = shift(block(3, True), "y", 4, -1)
    near_lo = shift(block(1, False), "y", 4, 1)
    via_lo = shift(add(block(3, False), far_lo), "y", 4, -1)
    via_hi = shift(add(block(1, True), far_hi), "y", 4, 1)
    parts = jnp.concatenate(
        [add(block(0, False), near_lo, via_lo), add(block(0, True), near_hi, via_hi)], axis=0
    ).reshape(NZ * NX, rows // (NZ * NX), piece)
    parts = lax.all_to_all(parts, ("z", "x"), split_axis=0, concat_axis=0, tiled=True)
    grad_factor = 1.0 / math.sqrt(TOK * NZ * NX * 8)
    mine = jnp.sum(parts.astype(f32), axis=0) * grad_factor
    mine = jnp.broadcast_to(mine[None], (8,) + mine.shape)
    blocks = lax.all_to_all(mine, ("core", "y"), split_axis=0, concat_axis=0, tiled=True)
    wo_grad = blocks.transpose(1, 0, 2).reshape(rows // (NZ * NX), width)

    layer_out = jnp.dot(attn_out, out_weight, preferred_element_type=f32).astype(bf16)
    k_grad = from_heads(kv_heads[:, :, :HEAD_DIM])
    v_grad = from_heads(kv_heads[:, :, HEAD_DIM:])
    return (layer_out, q_grad, k_grad, v_grad, wo_grad)


def solution(mesh):
    mesh = Mesh(mesh.devices.reshape(4, 2, NZ, NX), ("y", "core", "z", "x"))
    tokens = ("y", "core", "z", "x")
    placed = (
        P(tokens, None),
        P(tokens, None),
        P(tokens, None),
        P(tokens, None),
        P(),
        P(None, tokens, None),
    )
    return jax.shard_map(
        layer,
        mesh=mesh,
        in_specs=placed,
        out_specs=(
            P(tokens, None),
            P(tokens, None),
            P(tokens, None),
            P(tokens, None),
            P(("z", "x"), None),
        ),
        check_vma=False,
    )
```

```python
import functools
import math

import jax
import jax.numpy as jnp
from jax import lax
from jax.experimental import pallas as pl
from jax.experimental.pallas import tpu as pltpu
from jax.sharding import Mesh, PartitionSpec as P


HEADS = 8
HEAD_DIM = 128
CLUSTERS = 64
CAP = 8
TOK = 256
NZ = 8
NX = 4
SLOTS = CLUSTERS * CAP
META = 16
GROUP = 16
PAIR = 2 * HEAD_DIM
NEG_FILL = -1e30
X_STEP = (0, NX - 1, 1, 2)


def slot_row_of(meta):
    return meta[0:1, :] * CAP + meta[1:2, :]


def spread_rows(meta, rows):
    slot_iota = lax.broadcasted_iota(jnp.int32, (SLOTS, TOK), 0)
    hot = jnp.where(slot_iota == slot_row_of(meta).astype(jnp.int32), 1.0, 0.0).astype(jnp.bfloat16)
    out = jnp.dot(hot, rows, preferred_element_type=jnp.float32)
    return out.reshape(CLUSTERS, CAP, PAIR)


def spread_keys_kernel(base, *refs):
    *ins, slots, held, counts = refs
    for number, ref in enumerate(ins):
        pairs = ref.shape[0] // 2

        def some(z2, carry, ref=ref, first=number * pairs):
            got = []
            for i in range(2):
                z = 2 * z2 + i
                meta = ref[z, TOK : TOK + META, :].astype(jnp.float32)
                counts[pl.ds(2 * first + z, 1), :] = meta[2:3, :]
                got.append(spread_rows(meta, ref[z, 0:TOK, :]))
            slots[:, first + z2] = jnp.concatenate(got, axis=1).astype(jnp.bfloat16)
            return carry

        lax.fori_loop(0, pairs, some, 0)
    keys = 4 * NZ * CAP
    widen = jnp.where(
        lax.broadcasted_iota(jnp.int32, (NZ, keys), 1) // CAP
        == lax.broadcasted_iota(jnp.int32, (NZ, keys), 0) + base,
        1.0,
        0.0,
    )
    wide = lax.dot_general(
        counts[...], widen, (((0,), (0,)), ((), ())), preferred_element_type=jnp.float32
    )
    held[...] = wide[0:CLUSTERS, :]


def spread_queries_kernel(meta_lo, meta_hi, qg, slots):
    half = NZ // 4
    for ref, first in ((meta_lo, 0), (meta_hi, half)):

        def some(z2, carry, ref=ref, first=first):
            got = [
                spread_rows(ref[2 * z2 + i].astype(jnp.float32), qg[2 * (first + z2) + i])
                for i in range(2)
            ]
            slots[:, first + z2] = jnp.concatenate(got, axis=1).astype(jnp.bfloat16)
            return carry

        lax.fori_loop(0, half, some, 0)


def attend_kernel(
    x_ref, own, left, right, opp, qg, held_0, held_1, held_2, held_3,
    aq, d_own, d_left, d_right, d_opp, bias, causal,
):
    keys = 4 * NZ * CAP
    queries = NZ * CAP

    @pl.when(pl.program_id(0) == 0)
    def _():
        held = held_0[...] + held_1[...] + held_2[...] + held_3[...]
        lane = lax.broadcasted_iota(jnp.int32, (CLUSTERS, keys), 1) % CAP
        bias[...] = jnp.where(lane.astype(jnp.float32) < held, 0.0, NEG_FILL)
        me = x_ref[0]
        key_at = lax.broadcasted_iota(jnp.int32, (queries, keys), 1)
        source = key_at // (NZ * CAP)
        step = jnp.where(
            source == 1,
            X_STEP[1],
            jnp.where(source == 2, X_STEP[2], jnp.where(source == 3, X_STEP[3], 0)),
        )
        key_x = (me + step) % NX
        key_pos = (((key_at // CAP) % NZ) * NX + key_x) * CAP + key_at % CAP
        query_at = lax.broadcasted_iota(jnp.int32, (queries, keys), 0)
        query_pos = ((query_at // CAP) * NX + me) * CAP + query_at % CAP
        causal[...] = jnp.where(key_pos <= query_pos, 0.0, NEG_FILL)

    score_scale = HEAD_DIM ** (-0.5)
    zeros = jnp.zeros((queries, HEAD_DIM), jnp.bfloat16)
    first = pl.program_id(0) * GROUP
    many = range(GROUP)
    parts = (own, left, right, opp)
    kv = [
        jnp.concatenate([part[k].reshape(part.shape[1] * 2 * CAP, PAIR) for part in parts], axis=0)
        for k in many
    ]
    diag = []
    for k in many:
        qg_k = qg[k].reshape(queries, PAIR)
        diag.append(
            jnp.concatenate(
                [
                    jnp.concatenate([qg_k[:, :HEAD_DIM], zeros], axis=1),
                    jnp.concatenate([zeros, qg_k[:, HEAD_DIM:]], axis=1),
                ],
                axis=0,
            )
        )
    both = [
        lax.dot_general(
            diag[k], kv[k], (((1,), (1,)), ((), ())), preferred_element_type=jnp.float32
        )
        for k in many
    ]
    low = []
    for k in many:
        scores = both[k][:queries] * score_scale + (causal[...] + bias[pl.ds(first + k, 1), :])
        grad_prob = both[k][queries:]
        peak = jnp.max(scores, axis=-1, keepdims=True)
        terms = jnp.exp(scores - peak)
        weights = terms * (1.0 / jnp.sum(terms, axis=-1, keepdims=True))
        delta = jnp.sum(weights * grad_prob, axis=-1, keepdims=True)
        grad_score = weights * (grad_prob - delta) * score_scale
        low.append(
            jnp.concatenate(
                [grad_score.astype(jnp.bfloat16), weights.astype(jnp.bfloat16)], axis=0
            )
        )
    outs = [jnp.dot(low[k], kv[k], preferred_element_type=jnp.float32) for k in many]
    key_side = [
        lax.dot_general(
            low[k], diag[k], (((0,), (0,)), ((), ())), preferred_element_type=jnp.float32
        ).astype(jnp.bfloat16)
        for k in many
    ]
    for k in many:
        pair = jnp.concatenate([outs[k][queries:, HEAD_DIM:], outs[k][:queries, :HEAD_DIM]], axis=1)
        aq[k] = pair.astype(jnp.bfloat16).reshape(NZ // 2, 2 * CAP, PAIR)
        at = 0
        for ref in (d_own, d_left, d_right, d_opp):
            size = ref.shape[1] * 2 * CAP
            ref[k] = key_side[k][at : at + size].reshape(ref.shape[1], 2 * CAP, PAIR)
            at += size


def gather_kernel(meta_lo, meta_hi, slots, *outs):
    lane_iota = lax.broadcasted_iota(jnp.int32, (TOK, HEAD_DIM), 1).astype(jnp.float32)
    half = NZ // 4

    def hot_columns(meta):
        column = jnp.broadcast_to(slot_row_of(meta.astype(jnp.float32)), (HEAD_DIM, TOK)).T
        return jnp.concatenate(
            [
                jnp.where(column == lane_iota + float(HEAD_DIM * k), 1.0, 0.0).astype(jnp.bfloat16)
                for k in range(SLOTS // HEAD_DIM)
            ],
            axis=1,
        )

    for number, meta_in in enumerate((meta_lo, meta_hi)):
        out = outs[number % len(outs)]
        base = number * half
        shift_out = 2 * base if len(outs) == 1 else 0

        def step(z2, carry, out=out, base=base, meta_in=meta_in, shift_out=shift_out):
            wide = slots[:, base + z2].astype(jnp.float32)
            for i in range(2):
                rows = wide[:, i * CAP : (i + 1) * CAP, :].reshape(SLOTS, PAIR)
                got = jnp.dot(
                    hot_columns(meta_in[2 * z2 + i]),
                    rows.astype(jnp.bfloat16),
                    preferred_element_type=jnp.float32,
                )
                out[shift_out + 2 * z2 + i] = got.astype(jnp.bfloat16)
            return carry

        lax.fori_loop(0, half, step, 0)


VMEM = pl.BlockSpec(memory_space=pltpu.VMEM)
BF16 = jnp.bfloat16


def cost(flops, size):
    return pl.CostEstimate(flops=flops, bytes_accessed=size, transcendentals=0)


def spread_keys(base, lo, hi):
    ins = (lo, hi)
    return pl.pallas_call(
        functools.partial(spread_keys_kernel, base),
        out_shape=(
            jax.ShapeDtypeStruct((CLUSTERS, NZ // 2, 2 * CAP, PAIR), BF16),
            jax.ShapeDtypeStruct((CLUSTERS, 4 * NZ * CAP), jnp.float32),
        ),
        in_specs=[VMEM] * len(ins),
        out_specs=(VMEM, VMEM),
        scratch_shapes=[pltpu.VMEM((NZ, TOK), jnp.float32)],
        cost_estimate=cost(NZ << 26, NZ << 18),
        name="spread_keys",
    )(*ins)


def meta_spec():
    return pl.BlockSpec((NZ // 2, META, PAIR), lambda i: (0, TOK // META, 0))


def whole(shape):
    return pl.BlockSpec(shape, lambda i: (0,) * len(shape))


def spread_queries(lo, hi, qg):
    shape = (CLUSTERS, NZ // 2, 2 * CAP, PAIR)
    return pl.pallas_call(
        spread_queries_kernel,
        grid=(1,),
        out_shape=jax.ShapeDtypeStruct(shape, BF16),
        in_specs=[meta_spec(), meta_spec(), whole(qg.shape)],
        out_specs=whole(shape),
        cost_estimate=cost(NZ << 26, NZ << 18),
        name="spread_queries",
    )(lo, hi, qg)


def attend(x_index, slots, held, qg):
    def part(shape):
        return pl.BlockSpec((GROUP,) + shape[1:], lambda i: (i, 0, 0, 0))

    keys = 4 * NZ * CAP
    shapes = [qg.shape] + [s.shape for s in slots]
    return pl.pallas_call(
        attend_kernel,
        grid=(CLUSTERS // GROUP,),
        out_shape=[jax.ShapeDtypeStruct(s, BF16) for s in shapes],
        in_specs=[pl.BlockSpec(memory_space=pltpu.SMEM)]
        + [part(s.shape) for s in slots]
        + [part(qg.shape)]
        + [whole((CLUSTERS, keys))] * len(held),
        out_specs=[part(s) for s in shapes],
        scratch_shapes=[
            pltpu.VMEM((CLUSTERS, keys), jnp.float32),
            pltpu.VMEM((NZ * CAP, keys), jnp.float32),
        ],
        cost_estimate=cost(8 << 30, 20 << 20),
        name="attend",
    )(x_index, *slots, qg, *held)


def gather(pair, slots, halves):
    count = NZ // 2 if halves else NZ
    shapes = [(count, TOK, PAIR)] * (2 if halves else 1)
    return pl.pallas_call(
        gather_kernel,
        grid=(1,),
        out_shape=[jax.ShapeDtypeStruct(s, BF16) for s in shapes],
        in_specs=[meta_spec(), meta_spec(), whole(slots.shape)],
        out_specs=[whole(s) for s in shapes],
        cost_estimate=cost(NZ << 26, NZ << 18),
        name="gather_rows",
    )(*pair, slots)


def shift(value, axis, size, by):
    return lax.ppermute(value, axis, [(i, (i + by) % size) for i in range(size)])


def meta_rows(cluster_ids):
    f32 = jnp.float32
    ids = cluster_ids[:, :, 0]
    at = jnp.arange(TOK, dtype=jnp.int32)
    same = (ids[:, :, None] == ids[:, None, :]) & (at[:, None] < at[None, :])[None]
    rank = jnp.sum(same.astype(f32), axis=1)
    counts = jnp.sum((ids[:, :, None] == at[None, None, :]).astype(f32), axis=1)
    rows = jnp.stack([ids.astype(f32), rank, counts], axis=1)
    return jnp.pad(rows, ((0, 0), (0, META - 3), (0, 0))).astype(BF16)


def add(*terms):
    total = terms[0].astype(jnp.float32)
    for term in terms[1:]:
        total = total + term.astype(jnp.float32)
    return total.astype(BF16)


def layer(q_in, k_in, v_in, cotangent, out_weight, cluster_ids):
    f32, bf16 = jnp.float32, BF16
    half = NZ // 2

    def by_head(rows):
        return rows.reshape(TOK, HEADS, HEAD_DIM).transpose(1, 0, 2)

    def from_heads(rows):
        return rows.transpose(1, 0, 2).reshape(TOK, HEADS * HEAD_DIM)

    def swap_z(value):
        return lax.all_to_all(value, "z", split_axis=0, concat_axis=0, tiled=True)

    kv = jnp.concatenate(
        [jnp.concatenate([by_head(k_in), by_head(v_in)], axis=2), meta_rows(cluster_ids)], axis=1
    )
    kv = swap_z(kv)
    own = (kv[:half], kv[half:])
    left_lo = shift(own[0], "x", NX, 1)
    right_hi = shift(own[1], "x", NX, -1)
    left = (left_lo, shift(own[1], "x", NX, 1))
    right = (shift(own[0], "x", NX, -1), right_hi)
    opp = (shift(left_lo, "x", NX, 1), shift(right_hi, "x", NX, -1))
    grad_heads = lax.dot_general(
        cotangent, out_weight, (((1,), (1,)), ((), ())), preferred_element_type=f32
    ).astype(bf16)
    qg = swap_z(jnp.concatenate([by_head(q_in), by_head(grad_heads)], axis=2))
    columns = (own, left, right, opp)
    spread = []
    for number, pair in enumerate(columns):
        spread.append(spread_keys(number * NZ, *pair))
    qg_slots = spread_queries(*own, qg)
    x_index = lax.axis_index("x").reshape(1).astype(jnp.int32)
    aq, *d_slots = attend(x_index, [t[0] for t in spread], [t[1] for t in spread], qg_slots)

    (aq_rows,) = gather(own, aq, False)
    aq_heads = swap_z(aq_rows)
    sums = []
    for number, pair in enumerate(columns):
        sums.append(gather(pair, d_slots[number], True))
    own_d, left_d, right_d, opp_d = sums
    far_lo = shift(opp_d[0], "x", NX, -1)
    far_hi = shift(opp_d[1], "x", NX, 1)
    near_hi = shift(left_d[1], "x", NX, -1)
    near_lo = shift(right_d[0], "x", NX, 1)
    via_lo = shift(add(left_d[0], far_lo), "x", NX, -1)
    via_hi = shift(add(right_d[1], far_hi), "x", NX, 1)
    key_side = jnp.concatenate(
        [add(own_d[0], near_lo, via_lo), add(own_d[1], near_hi, via_hi)], axis=0
    )
    kv_heads = swap_z(key_side)

    attn_out = from_heads(aq_heads[:, :, :HEAD_DIM])
    q_grad = from_heads(aq_heads[:, :, HEAD_DIM:])

    y, core = lax.axis_index("y"), lax.axis_index("core")
    width = cotangent.shape[1]
    piece = width // 8
    rows = HEADS * HEAD_DIM

    def column_blocks(which):
        return jnp.concatenate(
            [
                lax.dynamic_slice_in_dim(
                    cotangent, which * (4 * piece) + ((y + r) % 4) * piece, piece, axis=1
                )
                for r in range(4)
            ],
            axis=1,
        )

    def weight_term(these):
        return lax.dot_general(
            attn_out, these, (((0,), (0,)), ((), ())), preferred_element_type=f32
        )

    other = shift(weight_term(column_blocks(1 - core)).astype(bf16), "core", 2, 1)
    term = (weight_term(column_blocks(core)) + other.astype(f32)).astype(bf16)

    def block(r, upper):
        here = term[:, r * piece : (r + 1) * piece]
        return here[rows // 2 :] if upper else here[: rows // 2]

    far_lo = shift(block(2, False), "y", 4, -1)
    far_hi = shift(block(2, True), "y", 4, 1)
    near_hi = shift(block(3, True), "y", 4, -1)
    near_lo = shift(block(1, False), "y", 4, 1)
    via_lo = shift(add(block(3, False), far_lo), "y", 4, -1)
    via_hi = shift(add(block(1, True), far_hi), "y", 4, 1)
    parts = jnp.concatenate(
        [add(block(0, False), near_lo, via_lo), add(block(0, True), near_hi, via_hi)], axis=0
    ).reshape(NZ * NX, rows // (NZ * NX), piece)
    parts = lax.all_to_all(parts, ("z", "x"), split_axis=0, concat_axis=0, tiled=True)
    grad_factor = 1.0 / math.sqrt(TOK * NZ * NX * 8)
    mine = jnp.sum(parts.astype(f32), axis=0) * grad_factor
    mine = jnp.broadcast_to(mine[None], (8,) + mine.shape)
    blocks = lax.all_to_all(mine, ("core", "y"), split_axis=0, concat_axis=0, tiled=True)
    wo_grad = blocks.transpose(1, 0, 2).reshape(rows // (NZ * NX), width)

    layer_out = jnp.dot(attn_out, out_weight, preferred_element_type=f32).astype(bf16)
    k_grad = from_heads(kv_heads[:, :, :HEAD_DIM])
    v_grad = from_heads(kv_heads[:, :, HEAD_DIM:])
    return (layer_out, q_grad, k_grad, v_grad, wo_grad)


def solution(mesh):
    mesh = Mesh(mesh.devices.reshape(4, 2, NZ, NX), ("y", "core", "z", "x"))
    tokens = ("y", "core", "z", "x")
    placed = (
        P(tokens, None),
        P(tokens, None),
        P(tokens, None),
        P(tokens, None),
        P(),
        P(None, tokens, None),
    )
    return jax.shard_map(
        layer,
        mesh=mesh,
        in_specs=placed,
        out_specs=(
            P(tokens, None),
            P(tokens, None),
            P(tokens, None),
            P(tokens, None),
            P(("z", "x"), None),
        ),
        check_vma=False,
    )
```

```python
import functools
import math

import jax
import jax.numpy as jnp
from jax import lax
from jax.experimental import pallas as pl
from jax.experimental.pallas import tpu as pltpu
from jax.sharding import Mesh, PartitionSpec as P


HEADS = 8
HEAD_DIM = 128
CLUSTERS = 64
CAP = 8
TOK = 256
NZ = 8
NX = 4
SLOTS = CLUSTERS * CAP
META = 16
GROUP = 16
PAIR = 2 * HEAD_DIM
NEG_FILL = -1e30
X_STEP = (0, NX - 1, 1, 2)


def slot_row_of(meta):
    return meta[0:1, :] * CAP + meta[1:2, :]


def spread_rows(meta, rows):
    slot_iota = lax.broadcasted_iota(jnp.int32, (SLOTS, TOK), 0)
    hot = jnp.where(slot_iota == slot_row_of(meta).astype(jnp.int32), 1.0, 0.0).astype(jnp.bfloat16)
    out = jnp.dot(hot, rows, preferred_element_type=jnp.float32)
    return out.reshape(CLUSTERS, CAP, PAIR)


def spread_keys_kernel(base, *refs):
    *ins, slots, held, counts = refs
    for number, ref in enumerate(ins):
        pairs = ref.shape[0] // 2

        def some(z2, carry, ref=ref, first=number * pairs):
            got = []
            for i in range(2):
                z = 2 * z2 + i
                meta = ref[z, TOK : TOK + META, :].astype(jnp.float32)
                counts[pl.ds(2 * first + z, 1), :] = meta[2:3, :]
                got.append(spread_rows(meta, ref[z, 0:TOK, :]))
            slots[:, first + z2] = jnp.concatenate(got, axis=1).astype(jnp.bfloat16)
            return carry

        lax.fori_loop(0, pairs, some, 0)
    keys = 4 * NZ * CAP
    widen = jnp.where(
        lax.broadcasted_iota(jnp.int32, (NZ, keys), 1) // CAP
        == lax.broadcasted_iota(jnp.int32, (NZ, keys), 0) + base,
        1.0,
        0.0,
    )
    wide = lax.dot_general(
        counts[...], widen, (((0,), (0,)), ((), ())), preferred_element_type=jnp.float32
    )
    held[...] = wide[0:CLUSTERS, :]


def spread_queries_kernel(meta_lo, meta_hi, qg, slots):
    half = NZ // 4
    for ref, first in ((meta_lo, 0), (meta_hi, half)):

        def some(z2, carry, ref=ref, first=first):
            got = [
                spread_rows(ref[2 * z2 + i].astype(jnp.float32), qg[2 * (first + z2) + i])
                for i in range(2)
            ]
            slots[:, first + z2] = jnp.concatenate(got, axis=1).astype(jnp.bfloat16)
            return carry

        lax.fori_loop(0, half, some, 0)


def attend_kernel(
    x_ref, own, left, right, opp, qg, held_0, held_1, held_2, held_3,
    aq, d_own, d_left, d_right, d_opp, bias, causal,
):
    keys = 4 * NZ * CAP
    queries = NZ * CAP

    @pl.when(pl.program_id(0) == 0)
    def _():
        held = held_0[...] + held_1[...] + held_2[...] + held_3[...]
        lane = lax.broadcasted_iota(jnp.int32, (CLUSTERS, keys), 1) % CAP
        bias[...] = jnp.where(lane.astype(jnp.float32) < held, 0.0, NEG_FILL)
        me = x_ref[0]
        key_at = lax.broadcasted_iota(jnp.int32, (queries, keys), 1)
        source = key_at // (NZ * CAP)
        step = jnp.where(
            source == 1,
            X_STEP[1],
            jnp.where(source == 2, X_STEP[2], jnp.where(source == 3, X_STEP[3], 0)),
        )
        key_x = (me + step) % NX
        key_pos = (((key_at // CAP) % NZ) * NX + key_x) * CAP + key_at % CAP
        query_at = lax.broadcasted_iota(jnp.int32, (queries, keys), 0)
        query_pos = ((query_at // CAP) * NX + me) * CAP + query_at % CAP
        causal[...] = jnp.where(key_pos <= query_pos, 0.0, NEG_FILL)

    score_scale = HEAD_DIM ** (-0.5)
    zeros = jnp.zeros((queries, HEAD_DIM), jnp.bfloat16)
    first = pl.program_id(0) * GROUP
    many = range(GROUP)
    parts = (own, left, right, opp)
    kv = [
        jnp.concatenate([part[k].reshape(part.shape[1] * 2 * CAP, PAIR) for part in parts], axis=0)
        for k in many
    ]
    diag = []
    for k in many:
        qg_k = qg[k].reshape(queries, PAIR)
        diag.append(
            jnp.concatenate(
                [
                    jnp.concatenate([qg_k[:, :HEAD_DIM], zeros], axis=1),
                    jnp.concatenate([zeros, qg_k[:, HEAD_DIM:]], axis=1),
                ],
                axis=0,
            )
        )
    both = [
        lax.dot_general(
            diag[k], kv[k], (((1,), (1,)), ((), ())), preferred_element_type=jnp.float32
        )
        for k in many
    ]
    low = []
    for k in many:
        scores = both[k][:queries] * score_scale + (causal[...] + bias[pl.ds(first + k, 1), :])
        grad_prob = both[k][queries:]
        peak = jnp.max(scores, axis=-1, keepdims=True)
        terms = jnp.exp(scores - peak)
        weights = terms * (1.0 / jnp.sum(terms, axis=-1, keepdims=True))
        delta = jnp.sum(weights * grad_prob, axis=-1, keepdims=True)
        grad_score = weights * (grad_prob - delta) * score_scale
        low.append(
            jnp.concatenate(
                [grad_score.astype(jnp.bfloat16), weights.astype(jnp.bfloat16)], axis=0
            )
        )
    outs = [jnp.dot(low[k], kv[k], preferred_element_type=jnp.float32) for k in many]
    key_side = [
        lax.dot_general(
            low[k], diag[k], (((0,), (0,)), ((), ())), preferred_element_type=jnp.float32
        ).astype(jnp.bfloat16)
        for k in many
    ]
    for k in many:
        pair = jnp.concatenate([outs[k][queries:, HEAD_DIM:], outs[k][:queries, :HEAD_DIM]], axis=1)
        aq[k] = pair.astype(jnp.bfloat16).reshape(NZ // 2, 2 * CAP, PAIR)
        at = 0
        for ref in (d_own, d_left, d_right, d_opp):
            size = ref.shape[1] * 2 * CAP
            ref[k] = key_side[k][at : at + size].reshape(ref.shape[1], 2 * CAP, PAIR)
            at += size


def gather_kernel(meta_lo, meta_hi, slots, *refs):
    *outs, metas = refs
    lane_iota = lax.broadcasted_iota(jnp.int32, (TOK, HEAD_DIM), 1).astype(jnp.float32)
    half = NZ // 4

    def hot_columns(meta):
        column = jnp.broadcast_to(slot_row_of(meta.astype(jnp.float32)), (HEAD_DIM, TOK)).T
        return jnp.concatenate(
            [
                jnp.where(column == lane_iota + float(HEAD_DIM * k), 1.0, 0.0).astype(jnp.bfloat16)
                for k in range(SLOTS // HEAD_DIM)
            ],
            axis=1,
        )

    metas[: NZ // 2] = meta_lo[...]
    metas[NZ // 2 :] = meta_hi[...]

    def step(z2, carry):
        wide = slots[:, z2].astype(jnp.float32)
        got = []
        for i in range(2):
            rows = wide[:, i * CAP : (i + 1) * CAP, :].reshape(SLOTS, PAIR)
            rows = jnp.dot(
                hot_columns(metas[2 * z2 + i]),
                rows.astype(jnp.bfloat16),
                preferred_element_type=jnp.float32,
            )
            got.append(rows.astype(jnp.bfloat16))
        if len(outs) == 1:
            for i in range(2):
                outs[0][2 * z2 + i] = got[i]
            return carry
        for number, out in enumerate(outs):

            @pl.when(z2 // half == number)
            def _(out=out, number=number):
                for i in range(2):
                    out[2 * (z2 - number * half) + i] = got[i]

        return carry

    lax.fori_loop(0, 2 * half, step, 0)


VMEM = pl.BlockSpec(memory_space=pltpu.VMEM)
BF16 = jnp.bfloat16


def cost(flops, size):
    return pl.CostEstimate(flops=flops, bytes_accessed=size, transcendentals=0)


def spread_keys(base, lo, hi):
    ins = (lo, hi)
    return pl.pallas_call(
        functools.partial(spread_keys_kernel, base),
        out_shape=(
            jax.ShapeDtypeStruct((CLUSTERS, NZ // 2, 2 * CAP, PAIR), BF16),
            jax.ShapeDtypeStruct((CLUSTERS, 4 * NZ * CAP), jnp.float32),
        ),
        in_specs=[VMEM] * len(ins),
        out_specs=(VMEM, VMEM),
        scratch_shapes=[pltpu.VMEM((NZ, TOK), jnp.float32)],
        cost_estimate=cost(NZ << 26, NZ << 18),
        name="spread_keys",
    )(*ins)


def meta_spec():
    return pl.BlockSpec((NZ // 2, META, PAIR), lambda i: (0, TOK // META, 0))


def whole(shape):
    return pl.BlockSpec(shape, lambda i: (0,) * len(shape))


def spread_queries(lo, hi, qg):
    shape = (CLUSTERS, NZ // 2, 2 * CAP, PAIR)
    return pl.pallas_call(
        spread_queries_kernel,
        grid=(1,),
        out_shape=jax.ShapeDtypeStruct(shape, BF16),
        in_specs=[meta_spec(), meta_spec(), whole(qg.shape)],
        out_specs=whole(shape),
        cost_estimate=cost(NZ << 26, NZ << 18),
        name="spread_queries",
    )(lo, hi, qg)


def attend(x_index, slots, held, qg):
    def part(shape):
        return pl.BlockSpec((GROUP,) + shape[1:], lambda i: (i, 0, 0, 0))

    keys = 4 * NZ * CAP
    shapes = [qg.shape] + [s.shape for s in slots]
    return pl.pallas_call(
        attend_kernel,
        grid=(CLUSTERS // GROUP,),
        out_shape=[jax.ShapeDtypeStruct(s, BF16) for s in shapes],
        in_specs=[pl.BlockSpec(memory_space=pltpu.SMEM)]
        + [part(s.shape) for s in slots]
        + [part(qg.shape)]
        + [whole((CLUSTERS, keys))] * len(held),
        out_specs=[part(s) for s in shapes],
        scratch_shapes=[
            pltpu.VMEM((CLUSTERS, keys), jnp.float32),
            pltpu.VMEM((NZ * CAP, keys), jnp.float32),
        ],
        cost_estimate=cost(8 << 30, 20 << 20),
        name="attend",
    )(x_index, *slots, qg, *held)


def gather(pair, slots, halves):
    count = NZ // 2 if halves else NZ
    shapes = [(count, TOK, PAIR)] * (2 if halves else 1)
    return pl.pallas_call(
        gather_kernel,
        grid=(1,),
        out_shape=[jax.ShapeDtypeStruct(s, BF16) for s in shapes],
        in_specs=[meta_spec(), meta_spec(), whole(slots.shape)],
        out_specs=[whole(s) for s in shapes],
        scratch_shapes=[pltpu.VMEM((NZ, META, PAIR), BF16)],
        cost_estimate=cost(NZ << 26, NZ << 18),
        name="gather_rows",
    )(*pair, slots)


def shift(value, axis, size, by):
    return lax.ppermute(value, axis, [(i, (i + by) % size) for i in range(size)])


def meta_rows(cluster_ids):
    f32 = jnp.float32
    ids = cluster_ids[:, :, 0]
    at = jnp.arange(TOK, dtype=jnp.int32)
    same = (ids[:, :, None] == ids[:, None, :]) & (at[:, None] < at[None, :])[None]
    rank = jnp.sum(same.astype(f32), axis=1)
    counts = jnp.sum((ids[:, :, None] == at[None, None, :]).astype(f32), axis=1)
    rows = jnp.stack([ids.astype(f32), rank, counts], axis=1)
    return jnp.pad(rows, ((0, 0), (0, META - 3), (0, 0))).astype(BF16)


def add(*terms):
    total = terms[0].astype(jnp.float32)
    for term in terms[1:]:
        total = total + term.astype(jnp.float32)
    return total.astype(BF16)


def layer(q_in, k_in, v_in, cotangent, out_weight, cluster_ids):
    f32, bf16 = jnp.float32, BF16
    half = NZ // 2

    def by_head(rows):
        return rows.reshape(TOK, HEADS, HEAD_DIM).transpose(1, 0, 2)

    def from_heads(rows):
        return rows.transpose(1, 0, 2).reshape(TOK, HEADS * HEAD_DIM)

    def swap_z(value):
        return lax.all_to_all(value, "z", split_axis=0, concat_axis=0, tiled=True)

    kv = jnp.concatenate(
        [jnp.concatenate([by_head(k_in), by_head(v_in)], axis=2), meta_rows(cluster_ids)], axis=1
    )
    kv = swap_z(kv)
    own = (kv[:half], kv[half:])
    left_lo = shift(own[0], "x", NX, 1)
    right_hi = shift(own[1], "x", NX, -1)
    left = (left_lo, shift(own[1], "x", NX, 1))
    right = (shift(own[0], "x", NX, -1), right_hi)
    opp = (shift(left_lo, "x", NX, 1), shift(right_hi, "x", NX, -1))
    grad_heads = lax.dot_general(
        cotangent, out_weight, (((1,), (1,)), ((), ())), preferred_element_type=f32
    ).astype(bf16)
    qg = swap_z(jnp.concatenate([by_head(q_in), by_head(grad_heads)], axis=2))
    columns = (own, left, right, opp)
    spread = []
    for number, pair in enumerate(columns):
        spread.append(spread_keys(number * NZ, *pair))
    qg_slots = spread_queries(*own, qg)
    x_index = lax.axis_index("x").reshape(1).astype(jnp.int32)
    aq, *d_slots = attend(x_index, [t[0] for t in spread], [t[1] for t in spread], qg_slots)

    (aq_rows,) = gather(own, aq, False)
    aq_heads = swap_z(aq_rows)
    sums = []
    for number, pair in enumerate(columns):
        sums.append(gather(pair, d_slots[number], True))
    own_d, left_d, right_d, opp_d = sums
    far_lo = shift(opp_d[0], "x", NX, -1)
    far_hi = shift(opp_d[1], "x", NX, 1)
    near_hi = shift(left_d[1], "x", NX, -1)
    near_lo = shift(right_d[0], "x", NX, 1)
    via_lo = shift(add(left_d[0], far_lo), "x", NX, -1)
    via_hi = shift(add(right_d[1], far_hi), "x", NX, 1)
    key_side = jnp.concatenate(
        [add(own_d[0], near_lo, via_lo), add(own_d[1], near_hi, via_hi)], axis=0
    )
    kv_heads = swap_z(key_side)

    attn_out = from_heads(aq_heads[:, :, :HEAD_DIM])
    q_grad = from_heads(aq_heads[:, :, HEAD_DIM:])

    y, core = lax.axis_index("y"), lax.axis_index("core")
    width = cotangent.shape[1]
    piece = width // 8
    rows = HEADS * HEAD_DIM

    def column_blocks(which):
        return jnp.concatenate(
            [
                lax.dynamic_slice_in_dim(
                    cotangent, which * (4 * piece) + ((y + r) % 4) * piece, piece, axis=1
                )
                for r in range(4)
            ],
            axis=1,
        )

    def weight_term(these):
        return lax.dot_general(
            attn_out, these, (((0,), (0,)), ((), ())), preferred_element_type=f32
        )

    other = shift(weight_term(column_blocks(1 - core)).astype(bf16), "core", 2, 1)
    term = (weight_term(column_blocks(core)) + other.astype(f32)).astype(bf16)

    def block(r, upper):
        here = term[:, r * piece : (r + 1) * piece]
        return here[rows // 2 :] if upper else here[: rows // 2]

    far_lo = shift(block(2, False), "y", 4, -1)
    far_hi = shift(block(2, True), "y", 4, 1)
    near_hi = shift(block(3, True), "y", 4, -1)
    near_lo = shift(block(1, False), "y", 4, 1)
    via_lo = shift(add(block(3, False), far_lo), "y", 4, -1)
    via_hi = shift(add(block(1, True), far_hi), "y", 4, 1)
    parts = jnp.concatenate(
        [add(block(0, False), near_lo, via_lo), add(block(0, True), near_hi, via_hi)], axis=0
    ).reshape(NZ, NX, rows // (NZ * NX), piece)
    x = lax.axis_index("x")

    def rows_for(r):
        return lax.dynamic_index_in_dim(parts, (x + r) % NX, axis=1, keepdims=False)

    from_one = shift(rows_for(1), "x", NX, 1)
    from_three = shift(rows_for(3), "x", NX, -1)
    from_two = shift(rows_for(2), "x", NX, 2)
    parts = add(rows_for(0), from_one, from_two, from_three)
    parts = swap_z(parts)
    grad_factor = 1.0 / math.sqrt(TOK * NZ * NX * 8)
    mine = jnp.sum(parts.astype(f32), axis=0) * grad_factor
    mine = jnp.broadcast_to(mine[None], (8,) + mine.shape)
    blocks = lax.all_to_all(mine, ("core", "y"), split_axis=0, concat_axis=0, tiled=True)
    wo_grad = blocks.transpose(1, 0, 2).reshape(rows // (NZ * NX), width)

    layer_out = jnp.dot(attn_out, out_weight, preferred_element_type=f32).astype(bf16)
    k_grad = from_heads(kv_heads[:, :, :HEAD_DIM])
    v_grad = from_heads(kv_heads[:, :, HEAD_DIM:])
    return (layer_out, q_grad, k_grad, v_grad, wo_grad)


def solution(mesh):
    mesh = Mesh(mesh.devices.reshape(4, 2, NZ, NX), ("y", "core", "z", "x"))
    tokens = ("y", "core", "z", "x")
    placed = (
        P(tokens, None),
        P(tokens, None),
        P(tokens, None),
        P(tokens, None),
        P(),
        P(None, tokens, None),
    )
    return jax.shard_map(
        layer,
        mesh=mesh,
        in_specs=placed,
        out_specs=(
            P(tokens, None),
            P(tokens, None),
            P(tokens, None),
            P(tokens, None),
            P(("z", "x"), None),
        ),
        check_vma=False,
    )
```

```python
import functools
import math

import jax
import jax.numpy as jnp
from jax import lax
from jax.experimental import pallas as pl
from jax.experimental.pallas import tpu as pltpu
from jax.sharding import Mesh, PartitionSpec as P


HEADS = 8
HEAD_DIM = 128
CLUSTERS = 64
CAP = 8
TOK = 256
NZ = 8
NX = 4
SLOTS = CLUSTERS * CAP
META = 16
GROUP = 16
PAIR = 2 * HEAD_DIM
NEG_FILL = -1e30
X_STEP = (0, NX - 1, 1, 2)


def slot_row_of(meta):
    return meta[0:1, :] * CAP + meta[1:2, :]


def spread_rows(meta, rows):
    slot_iota = lax.broadcasted_iota(jnp.int32, (SLOTS, TOK), 0)
    hot = jnp.where(slot_iota == slot_row_of(meta).astype(jnp.int32), 1.0, 0.0).astype(jnp.bfloat16)
    out = jnp.dot(hot, rows, preferred_element_type=jnp.float32)
    return out.reshape(CLUSTERS, CAP, PAIR)


def spread_keys_kernel(base, *refs):
    *ins, slots, held, counts = refs
    for number, ref in enumerate(ins):
        pairs = ref.shape[0] // 2

        def some(z2, carry, ref=ref, first=number * pairs):
            got = []
            for i in range(2):
                z = 2 * z2 + i
                meta = ref[z, TOK : TOK + META, :].astype(jnp.float32)
                counts[pl.ds(2 * first + z, 1), :] = meta[2:3, :]
                got.append(spread_rows(meta, ref[z, 0:TOK, :]))
            slots[:, first + z2] = jnp.concatenate(got, axis=1).astype(jnp.bfloat16)
            return carry

        lax.fori_loop(0, pairs, some, 0, unroll=base == 3 * NZ)
    keys = 4 * NZ * CAP
    widen = jnp.where(
        lax.broadcasted_iota(jnp.int32, (NZ, keys), 1) // CAP
        == lax.broadcasted_iota(jnp.int32, (NZ, keys), 0) + base,
        1.0,
        0.0,
    )
    wide = lax.dot_general(
        counts[...], widen, (((0,), (0,)), ((), ())), preferred_element_type=jnp.float32
    )
    held[...] = wide[0:CLUSTERS, :]


def spread_queries_kernel(meta_lo, meta_hi, qg, slots):
    half = NZ // 4
    for ref, first in ((meta_lo, 0), (meta_hi, half)):

        def some(z2, carry, ref=ref, first=first):
            got = [
                spread_rows(ref[2 * z2 + i].astype(jnp.float32), qg[2 * (first + z2) + i])
                for i in range(2)
            ]
            slots[:, first + z2] = jnp.concatenate(got, axis=1).astype(jnp.bfloat16)
            return carry

        lax.fori_loop(0, half, some, 0, unroll=True)


def attend_kernel(
    x_ref, own, left, right, opp, qg, held_0, held_1, held_2, held_3,
    aq, d_own, d_left, d_right, d_opp, bias, causal,
):
    keys = 4 * NZ * CAP
    queries = NZ * CAP

    @pl.when(pl.program_id(0) == 0)
    def _():
        held = held_0[...] + held_1[...] + held_2[...] + held_3[...]
        lane = lax.broadcasted_iota(jnp.int32, (CLUSTERS, keys), 1) % CAP
        bias[...] = jnp.where(lane.astype(jnp.float32) < held, 0.0, NEG_FILL)
        me = x_ref[0]
        key_at = lax.broadcasted_iota(jnp.int32, (queries, keys), 1)
        source = key_at // (NZ * CAP)
        step = jnp.where(
            source == 1,
            X_STEP[1],
            jnp.where(source == 2, X_STEP[2], jnp.where(source == 3, X_STEP[3], 0)),
        )
        key_x = (me + step) % NX
        key_pos = (((key_at // CAP) % NZ) * NX + key_x) * CAP + key_at % CAP
        query_at = lax.broadcasted_iota(jnp.int32, (queries, keys), 0)
        query_pos = ((query_at // CAP) * NX + me) * CAP + query_at % CAP
        causal[...] = jnp.where(key_pos <= query_pos, 0.0, NEG_FILL)

    score_scale = HEAD_DIM ** (-0.5)
    zeros = jnp.zeros((queries, HEAD_DIM), jnp.bfloat16)
    first = pl.program_id(0) * GROUP
    many = range(GROUP)
    parts = (own, left, right, opp)
    kv = [
        jnp.concatenate([part[k].reshape(part.shape[1] * 2 * CAP, PAIR) for part in parts], axis=0)
        for k in many
    ]
    diag = []
    for k in many:
        qg_k = qg[k].reshape(queries, PAIR)
        diag.append(
            jnp.concatenate(
                [
                    jnp.concatenate([qg_k[:, :HEAD_DIM], zeros], axis=1),
                    jnp.concatenate([zeros, qg_k[:, HEAD_DIM:]], axis=1),
                ],
                axis=0,
            )
        )
    both = [
        lax.dot_general(
            diag[k], kv[k], (((1,), (1,)), ((), ())), preferred_element_type=jnp.float32
        )
        for k in many
    ]
    low = []
    for k in many:
        scores = both[k][:queries] * score_scale + (causal[...] + bias[pl.ds(first + k, 1), :])
        grad_prob = both[k][queries:]
        peak = jnp.max(scores, axis=-1, keepdims=True)
        terms = jnp.exp(scores - peak)
        weights = terms * (1.0 / jnp.sum(terms, axis=-1, keepdims=True))
        delta = jnp.sum(weights * grad_prob, axis=-1, keepdims=True)
        grad_score = weights * (grad_prob - delta) * score_scale
        low.append(
            jnp.concatenate(
                [grad_score.astype(jnp.bfloat16), weights.astype(jnp.bfloat16)], axis=0
            )
        )
    outs = [jnp.dot(low[k], kv[k], preferred_element_type=jnp.float32) for k in many]
    key_side = [
        lax.dot_general(
            low[k], diag[k], (((0,), (0,)), ((), ())), preferred_element_type=jnp.float32
        ).astype(jnp.bfloat16)
        for k in many
    ]
    for k in many:
        pair = jnp.concatenate([outs[k][queries:, HEAD_DIM:], outs[k][:queries, :HEAD_DIM]], axis=1)
        aq[k] = pair.astype(jnp.bfloat16).reshape(NZ // 2, 2 * CAP, PAIR)
        at = 0
        for ref in (d_own, d_left, d_right, d_opp):
            size = ref.shape[1] * 2 * CAP
            ref[k] = key_side[k][at : at + size].reshape(ref.shape[1], 2 * CAP, PAIR)
            at += size


def gather_kernel(unroll, meta_lo, meta_hi, slots, *outs):
    lane_iota = lax.broadcasted_iota(jnp.int32, (TOK, HEAD_DIM), 1).astype(jnp.float32)
    half = NZ // 4

    def hot_columns(meta):
        column = jnp.broadcast_to(slot_row_of(meta.astype(jnp.float32)), (HEAD_DIM, TOK)).T
        return jnp.concatenate(
            [
                jnp.where(column == lane_iota + float(HEAD_DIM * k), 1.0, 0.0).astype(jnp.bfloat16)
                for k in range(SLOTS // HEAD_DIM)
            ],
            axis=1,
        )

    for number, meta_in in enumerate((meta_lo, meta_hi)):
        out = outs[number % len(outs)]
        base = number * half
        shift_out = 2 * base if len(outs) == 1 else 0

        def step(z2, carry, out=out, base=base, meta_in=meta_in, shift_out=shift_out):
            wide = slots[:, base + z2].astype(jnp.float32)
            for i in range(2):
                rows = wide[:, i * CAP : (i + 1) * CAP, :].reshape(SLOTS, PAIR)
                got = jnp.dot(
                    hot_columns(meta_in[2 * z2 + i]),
                    rows.astype(jnp.bfloat16),
                    preferred_element_type=jnp.float32,
                )
                out[shift_out + 2 * z2 + i] = got.astype(jnp.bfloat16)
            return carry

        lax.fori_loop(0, half, step, 0, unroll=unroll)


VMEM = pl.BlockSpec(memory_space=pltpu.VMEM)
BF16 = jnp.bfloat16


def cost(flops, size):
    return pl.CostEstimate(flops=flops, bytes_accessed=size, transcendentals=0)


def spread_keys(base, lo, hi):
    ins = (lo, hi)
    return pl.pallas_call(
        functools.partial(spread_keys_kernel, base),
        out_shape=(
            jax.ShapeDtypeStruct((CLUSTERS, NZ // 2, 2 * CAP, PAIR), BF16),
            jax.ShapeDtypeStruct((CLUSTERS, 4 * NZ * CAP), jnp.float32),
        ),
        in_specs=[VMEM] * len(ins),
        out_specs=(VMEM, VMEM),
        scratch_shapes=[pltpu.VMEM((NZ, TOK), jnp.float32)],
        cost_estimate=cost(NZ << 26, NZ << 18),
        name="spread_keys",
    )(*ins)


def meta_spec():
    return pl.BlockSpec((NZ // 2, META, PAIR), lambda i: (0, TOK // META, 0))


def whole(shape):
    return pl.BlockSpec(shape, lambda i: (0,) * len(shape))


def spread_queries(lo, hi, qg):
    shape = (CLUSTERS, NZ // 2, 2 * CAP, PAIR)
    return pl.pallas_call(
        spread_queries_kernel,
        grid=(1,),
        out_shape=jax.ShapeDtypeStruct(shape, BF16),
        in_specs=[meta_spec(), meta_spec(), whole(qg.shape)],
        out_specs=whole(shape),
        cost_estimate=cost(NZ << 26, NZ << 18),
        name="spread_queries",
    )(lo, hi, qg)


def attend(x_index, slots, held, qg):
    def part(shape):
        return pl.BlockSpec((GROUP,) + shape[1:], lambda i: (i, 0, 0, 0))

    keys = 4 * NZ * CAP
    shapes = [qg.shape] + [s.shape for s in slots]
    return pl.pallas_call(
        attend_kernel,
        grid=(CLUSTERS // GROUP,),
        out_shape=[jax.ShapeDtypeStruct(s, BF16) for s in shapes],
        in_specs=[pl.BlockSpec(memory_space=pltpu.SMEM)]
        + [part(s.shape) for s in slots]
        + [part(qg.shape)]
        + [whole((CLUSTERS, keys))] * len(held),
        out_specs=[part(s) for s in shapes],
        scratch_shapes=[
            pltpu.VMEM((CLUSTERS, keys), jnp.float32),
            pltpu.VMEM((NZ * CAP, keys), jnp.float32),
        ],
        cost_estimate=cost(8 << 30, 20 << 20),
        name="attend",
    )(x_index, *slots, qg, *held)


def gather(pair, slots, halves, unroll=False):
    count = NZ // 2 if halves else NZ
    shapes = [(count, TOK, PAIR)] * (2 if halves else 1)
    return pl.pallas_call(
        functools.partial(gather_kernel, unroll),
        grid=(1,),
        out_shape=[jax.ShapeDtypeStruct(s, BF16) for s in shapes],
        in_specs=[meta_spec(), meta_spec(), whole(slots.shape)],
        out_specs=[whole(s) for s in shapes],
        cost_estimate=cost(NZ << 26, NZ << 18),
        name="gather_rows",
    )(*pair, slots)


def shift(value, axis, size, by):
    return lax.ppermute(value, axis, [(i, (i + by) % size) for i in range(size)])


def meta_rows(cluster_ids):
    f32 = jnp.float32
    ids = cluster_ids[:, :, 0]
    at = jnp.arange(TOK, dtype=jnp.int32)
    same = (ids[:, :, None] == ids[:, None, :]) & (at[:, None] < at[None, :])[None]
    rank = jnp.sum(same.astype(f32), axis=1)
    counts = jnp.sum((ids[:, :, None] == at[None, None, :]).astype(f32), axis=1)
    rows = jnp.stack([ids.astype(f32), rank, counts], axis=1)
    return jnp.pad(rows, ((0, 0), (0, META - 3), (0, 0))).astype(BF16)


def add(*terms):
    total = terms[0].astype(jnp.float32)
    for term in terms[1:]:
        total = total + term.astype(jnp.float32)
    return total.astype(BF16)


def layer(q_in, k_in, v_in, cotangent, out_weight, cluster_ids):
    f32, bf16 = jnp.float32, BF16
    half = NZ // 2

    def by_head(rows):
        return rows.reshape(TOK, HEADS, HEAD_DIM).transpose(1, 0, 2)

    def from_heads(rows):
        return rows.transpose(1, 0, 2).reshape(TOK, HEADS * HEAD_DIM)

    def swap_z(value):
        return lax.all_to_all(value, "z", split_axis=0, concat_axis=0, tiled=True)

    kv = jnp.concatenate(
        [jnp.concatenate([by_head(k_in), by_head(v_in)], axis=2), meta_rows(cluster_ids)], axis=1
    )
    kv = swap_z(kv)
    own = (kv[:half], kv[half:])
    left_lo = shift(own[0], "x", NX, 1)
    right_hi = shift(own[1], "x", NX, -1)
    left = (left_lo, shift(own[1], "x", NX, 1))
    right = (shift(own[0], "x", NX, -1), right_hi)
    opp = (shift(left_lo, "x", NX, 1), shift(right_hi, "x", NX, -1))
    grad_heads = lax.dot_general(
        cotangent, out_weight, (((1,), (1,)), ((), ())), preferred_element_type=f32
    ).astype(bf16)
    qg = swap_z(jnp.concatenate([by_head(q_in), by_head(grad_heads)], axis=2))
    columns = (own, left, right, opp)
    spread = []
    for number, pair in enumerate(columns):
        spread.append(spread_keys(number * NZ, *pair))
    qg_slots = spread_queries(*own, qg)
    x_index = lax.axis_index("x").reshape(1).astype(jnp.int32)
    aq, *d_slots = attend(x_index, [t[0] for t in spread], [t[1] for t in spread], qg_slots)

    (aq_rows,) = gather(own, aq, False, True)
    aq_heads = swap_z(aq_rows)
    sums = []
    for number, pair in enumerate(columns):
        sums.append(gather(pair, d_slots[number], True, number == 3))
    own_d, left_d, right_d, opp_d = sums
    far_lo = shift(opp_d[0], "x", NX, -1)
    far_hi = shift(opp_d[1], "x", NX, 1)
    near_hi = shift(left_d[1], "x", NX, -1)
    near_lo = shift(right_d[0], "x", NX, 1)
    via_lo = shift(add(left_d[0], far_lo), "x", NX, -1)
    via_hi = shift(add(right_d[1], far_hi), "x", NX, 1)
    key_side = jnp.concatenate(
        [add(own_d[0], near_lo, via_lo), add(own_d[1], near_hi, via_hi)], axis=0
    )
    kv_heads = swap_z(key_side)

    attn_out = from_heads(aq_heads[:, :, :HEAD_DIM])
    q_grad = from_heads(aq_heads[:, :, HEAD_DIM:])

    y, core = lax.axis_index("y"), lax.axis_index("core")
    width = cotangent.shape[1]
    piece = width // 8
    rows = HEADS * HEAD_DIM

    def column_blocks(which):
        return jnp.concatenate(
            [
                lax.dynamic_slice_in_dim(
                    cotangent, which * (4 * piece) + ((y + r) % 4) * piece, piece, axis=1
                )
                for r in range(4)
            ],
            axis=1,
        )

    def weight_term(these):
        return lax.dot_general(
            attn_out, these, (((0,), (0,)), ((), ())), preferred_element_type=f32
        )

    other = shift(weight_term(column_blocks(1 - core)).astype(bf16), "core", 2, 1)
    term = (weight_term(column_blocks(core)) + other.astype(f32)).astype(bf16)

    def block(r, upper):
        here = term[:, r * piece : (r + 1) * piece]
        return here[rows // 2 :] if upper else here[: rows // 2]

    far_lo = shift(block(2, False), "y", 4, -1)
    far_hi = shift(block(2, True), "y", 4, 1)
    near_hi = shift(block(3, True), "y", 4, -1)
    near_lo = shift(block(1, False), "y", 4, 1)
    via_lo = shift(add(block(3, False), far_lo), "y", 4, -1)
    via_hi = shift(add(block(1, True), far_hi), "y", 4, 1)
    parts = jnp.concatenate(
        [add(block(0, False), near_lo, via_lo), add(block(0, True), near_hi, via_hi)], axis=0
    ).reshape(NZ * NX, rows // (NZ * NX), piece)
    parts = lax.all_to_all(parts, ("z", "x"), split_axis=0, concat_axis=0, tiled=True)
    grad_factor = 1.0 / math.sqrt(TOK * NZ * NX * 8)
    mine = jnp.sum(parts.astype(f32), axis=0) * grad_factor
    mine = jnp.broadcast_to(mine[None], (8,) + mine.shape)
    blocks = lax.all_to_all(mine, ("core", "y"), split_axis=0, concat_axis=0, tiled=True)
    wo_grad = blocks.transpose(1, 0, 2).reshape(rows // (NZ * NX), width)

    layer_out = jnp.dot(attn_out, out_weight, preferred_element_type=f32).astype(bf16)
    k_grad = from_heads(kv_heads[:, :, :HEAD_DIM])
    v_grad = from_heads(kv_heads[:, :, HEAD_DIM:])
    return (layer_out, q_grad, k_grad, v_grad, wo_grad)


def solution(mesh):
    mesh = Mesh(mesh.devices.reshape(4, 2, NZ, NX), ("y", "core", "z", "x"))
    tokens = ("y", "core", "z", "x")
    placed = (
        P(tokens, None),
        P(tokens, None),
        P(tokens, None),
        P(tokens, None),
        P(),
        P(None, tokens, None),
    )
    return jax.shard_map(
        layer,
        mesh=mesh,
        in_specs=placed,
        out_specs=(
            P(tokens, None),
            P(tokens, None),
            P(tokens, None),
            P(tokens, None),
            P(("z", "x"), None),
        ),
        check_vma=False,
    )
```
